32 devices in a mesh: facet: 8 (over y, x, core), pix: 4 (over z).
Axes of the slice: x: 2, y: 2, z: 4, core: 2. Of those that a mesh axis runs over, the one named last changes fastest.
Arguments:
- image: float32 [32, 512, 512], P(('facet', 'pix')), may hold values from 0 to 1
- visibilities: float32 [2, 32, 256, 128], P(None, ('facet', 'pix')), may hold values from -6 to 6
- tile_index: int32 [32, 256], P(('facet', 'pix')), may hold values from 0 to 1023
- cells: int32 [32, 256, 128], P(('facet', 'pix')), may hold values from 0 to 1023
- block_count: int32 [32], P(('facet', 'pix')), may hold values from 64 to 256, as said below
- lowrank_dual: float32 [32, 512, 512], P(None, ('facet', 'pix')), may hold values from -6 to 6
- wavelet_dual: float32 [32, 512, 512], P(None, ('facet', 'pix')), may hold values from -4 to 4
- wavelet_bound: float32 [32], replicated, may hold values from 0.2 to 2
Outputs:
- image_next: float32 [32, 512, 512], P(('facet', 'pix'))
- lowrank_next: float32 [32, 512, 512], P(None, ('facet', 'pix'))
- wavelet_next: float32 [32, 512, 512], P(None, ('facet', 'pix'))
The draws below stay inside these ranges and needn't reach their ends.
Inputs may be any that keep to these rules, and one draw needn't show every extreme that they name: `cells`: cell within the tile is its row times 128 plus its column. `block_count`: blocks at or after a channel's count are padding; some channel has all 256 blocks live.
All inputs are finite; a program needn't handle non-finite values.
Results may differ from the reference program's by a relative error of at most 0.0003.
Values sent between devices are 32-bit elements; how exact they have to be, the bound alone decides.
No kernel may reach another device: no remote copies, remote signals or barrier semaphores. Data moves between devices by JAX's collectives and lax.ppermute only.
A program may use at most 128 MiB of HBM per device.

```python
import math
import jax
import jax.numpy as jnp
from jax import lax

IMG = 512
COLS = 512
GRID_R = 1024
GRID_C = 1024
TILE_R = 8
TILE_C = 128
NTILES = 1024
NBLK = 256
VB = 128
NS_STEPS = 5
CHANNELS = 32
FACET_PIX = 32768
N_FACET = 8


def draw_block_count(key, part):
    first_key, second_key = jax.random.split(jax.random.fold_in(key, 17))
    counts = jax.random.randint(first_key, (CHANNELS,), NBLK // 4, NBLK + 1)
    chosen = jax.random.randint(second_key, (), 0, CHANNELS)
    return jnp.where(jnp.arange(CHANNELS) == chosen, NBLK, counts).astype(jnp.int32)


def place_ends(drawn, rng, least, high):
    index_at = [jax.random.randint(jax.random.fold_in(rng, axis), (), 0, length) for axis, length in enumerate(drawn.shape)]
    longest = drawn.shape.index(max(drawn.shape))
    beside = index_at[:longest] + [(index_at[longest] + 1) % drawn.shape[longest]] + index_at[longest + 1:]
    return drawn.at[tuple(index_at)].set(least).at[tuple(beside)].set(high)


def shard_levels(rng, extent, cuts, least, top_value):
    loudness = 1.0
    for axis_at, shards_of in cuts:
        draws = jax.random.uniform(jax.random.fold_in(jax.random.fold_in(rng, 6), axis_at), (shards_of,), jnp.float32, least / len(cuts), top_value / len(cuts))
        loudness = loudness * jnp.repeat(jnp.exp(draws), extent[axis_at] // shards_of).reshape((-1,) + (1,) * (len(extent) - 1 - axis_at))
    return loudness


def centred(key, dims, scale, most, cuts=(), held_as=jnp.bfloat16):
    drawn = scale * jax.random.normal(key, dims, jnp.float32)
    if cuts:
        drawn = drawn * shard_levels(key, dims, cuts, -0.22, 0.18)
    return jnp.clip(drawn, -most, most).astype(held_as)


def setup_inputs(seed: int = 0) -> dict:
    keys = jax.random.split(jax.random.key(seed), 9)
    return {
        "image": jnp.clip(1.0 * jax.random.uniform(keys[0], (CHANNELS, IMG, COLS), jnp.float32) ** shard_levels(keys[0], (CHANNELS, IMG, COLS), ((0, 32),), -0.2, 0.2), 0.0, 1.0),
        "visibilities": centred(keys[1], (2, CHANNELS, NBLK, VB), 1.0, 6.0, ((1, 32),), jnp.float32),
        "tile_index": place_ends(jax.random.randint(keys[2], (CHANNELS, NBLK), 0, NTILES), jax.random.fold_in(keys[2], 1), 0, NTILES - 1).astype(jnp.int32),
        "cells": place_ends(jax.random.randint(keys[3], (CHANNELS, NBLK, VB), 0, TILE_R * TILE_C), jax.random.fold_in(keys[3], 1), 0, (TILE_R * TILE_C) - 1).astype(jnp.int32),
        "block_count": draw_block_count(jax.random.fold_in(keys[8], 71), 0),
        "lowrank_dual": centred(keys[5], (CHANNELS, IMG, COLS), 1.0, 6.0, ((1, 32),), jnp.float32),
        "wavelet_dual": centred(keys[6], (CHANNELS, IMG, COLS), 0.5, 4.0, ((1, 32),), jnp.float32),
        "wavelet_bound": jnp.clip(jnp.exp(jax.random.uniform(keys[7], (CHANNELS,), jnp.float32, math.log(0.2), math.log(2.0))), 0.2, 2.0),
    }


highest = lax.Precision.HIGHEST
tau_step = 0.5
sigma_step = 1.0

def kernel_weights(cells):
    row_pos = (cells // TILE_C).astype(jnp.float32)
    col_pos = (cells % TILE_C).astype(jnp.float32)
    row_gap = jnp.arange(TILE_R, dtype=jnp.float32) - row_pos[..., None]
    col_gap = jnp.arange(TILE_C, dtype=jnp.float32) - col_pos[..., None]
    return (jnp.exp(-0.5 * row_gap * row_gap), jnp.exp(-0.5 * col_gap * col_gap))

def channel_gradient(items):
    plane, vis_pair, tiles, cells, count = items
    padded = jnp.zeros((GRID_R, GRID_C), jnp.float32).at[:IMG, :COLS].set(plane)
    spectrum = jnp.fft.fft2(padded) / IMG
    grid_pair = jnp.stack([jnp.real(spectrum), jnp.imag(spectrum)]).astype(jnp.float32)
    tiled = grid_pair.reshape(2, GRID_R // TILE_R, TILE_R, GRID_C // TILE_C, TILE_C).transpose(0, 1, 3, 2, 4)
    tiled = tiled.reshape(2, NTILES, TILE_R, TILE_C)
    picked = tiled[:, tiles]
    along_rows, along_cols = kernel_weights(cells)
    partial_sum = jnp.einsum('kvj,pkij->pkvi', along_cols, picked, precision=highest)
    model = lax.optimization_barrier(jnp.sum(partial_sum * along_rows[None], axis=-1))
    live = (jnp.arange(NBLK, dtype=jnp.int32) < count).astype(jnp.float32)
    misfit = (model - vis_pair) * live[None, :, None]
    spread = jnp.einsum('pkvi,kvj->pkij', misfit[..., None] * along_rows[None], along_cols, precision=highest)
    gridded = jnp.zeros((2, NTILES, TILE_R, TILE_C), jnp.float32).at[:, tiles].add(spread)
    full = gridded.reshape(2, GRID_R // TILE_R, GRID_C // TILE_C, TILE_R, TILE_C).transpose(0, 1, 3, 2, 4)
    full = full.reshape(2, GRID_R, GRID_C)
    back = jnp.fft.ifft2(full[0] + 1j * full[1]) * (GRID_R * GRID_C)
    return jnp.real(back)[:IMG, :COLS].astype(jnp.float32) / IMG

def inverse_root(gram, ridge):
    identity = jnp.eye(gram.shape[0], dtype=jnp.float32)
    shifted = gram + ridge * identity
    total = jnp.trace(shifted)
    current = shifted / total
    inverse = identity
    for turn in range(NS_STEPS):
        factor = 1.5 * identity - 0.5 * jnp.dot(inverse, current, precision=highest)
        current = jnp.dot(current, factor, precision=highest)
        inverse = jnp.dot(factor, inverse, precision=highest)
    return inverse / jnp.sqrt(total)

def row_difference(field):
    padded = jnp.pad(field, ((0, 0), (1, 1), (0, 0)))
    return padded[:, 1:-1] - 0.5 * (padded[:, :-2] + padded[:, 2:])

def column_difference(field):
    padded = jnp.pad(field, ((0, 0), (0, 0), (1, 1)))
    return padded[:, :, 1:-1] - 0.5 * (padded[:, :, :-2] + padded[:, :, 2:])

def detail(field):
    return column_difference(row_difference(field))

def reference(image, visibilities, tile_index, cells, block_count, lowrank_dual, wavelet_dual, wavelet_bound):
    gradient = lax.map(channel_gradient, (image, jnp.moveaxis(visibilities, 1, 0), tile_index, cells, block_count))
    lifted = lowrank_dual + sigma_step * image
    facets = lifted.reshape(CHANNELS, N_FACET, FACET_PIX).transpose(1, 0, 2)

    def facet_update(block):
        gram = jnp.dot(block, block.T, precision=highest)
        root = inverse_root(gram, float(FACET_PIX))
        return math.sqrt(FACET_PIX) * jnp.dot(root, block, precision=highest)
    lowrank_next = lax.map(facet_update, facets).transpose(1, 0, 2).reshape(CHANNELS, IMG, COLS)
    bound = wavelet_bound[:, None, None]
    wavelet_next = jnp.clip(wavelet_dual + sigma_step * detail(image), -bound, bound)
    direction = 2.0 * lowrank_next - lowrank_dual + detail(2.0 * wavelet_next - wavelet_dual)
    image_next = jnp.maximum(image - tau_step * (gradient + direction), 0.0)
    return (image_next, lowrank_next, wavelet_next)
```

```python
import functools
import math

import jax
import jax.numpy as jnp
import numpy as np
from jax import lax
from jax.experimental import pallas as pl
from jax.experimental.pallas import tpu as pltpu
from jax.sharding import PartitionSpec as P

TILE_R = 8
TILE_C = 128
NS_STEPS = 5
GROUP = 16
RING = ("facet", "pix")

highest = lax.Precision.HIGHEST
tau_step = 0.5
sigma_step = 1.0
f32 = jnp.float32
bf16 = jnp.bfloat16
VMEM_BYTES = 56 * 1024 * 1024


def gauss(n):
    d = np.arange(n)[:, None] - np.arange(n)[None, :]
    return np.exp(-0.5 * d.astype(np.float64) ** 2)


def small_tables(height, width):
    rows, cols = 2 * height, 2 * width
    m = np.arange(height)
    n = np.arange(width)
    near = gauss(TILE_R) @ np.exp(-2j * np.pi * np.arange(TILE_R)[:, None] * m[None, :] / rows)
    period = rows // TILE_R
    turn = np.exp(
        -2j * np.pi * (np.arange(period)[:, None] * np.arange(period)[None, :] % period) / period
    )
    span = np.exp(-2j * np.pi * n[:, None] * np.arange(TILE_C)[None, :] / cols) @ gauss(TILE_C)
    span = span / height
    bands = cols // TILE_C
    swing = np.exp(-2j * np.pi * np.arange(bands)[:, None] * np.arange(8)[None, :] / bands)
    swing = np.broadcast_to(swing[:, :, None], (bands, 8, TILE_C))
    assert bands == 8 and period == 128
    out = []
    for table in (near, turn, span, swing):
        out += [np.ascontiguousarray(table.real, np.float32), np.ascontiguousarray(table.imag, np.float32)]
    return out


def split(x):
    high = x.astype(bf16)
    return high, (x - high.astype(f32)).astype(bf16)


def dot3(a_hi, a_lo, b_hi, b_lo):
    return (
        jnp.dot(a_hi, b_hi, preferred_element_type=f32)
        + jnp.dot(a_lo, b_hi, preferred_element_type=f32)
        + jnp.dot(a_hi, b_lo, preferred_element_type=f32)
    )


def nt(a, b):
    return lax.dot_general(a, b, (((1,), (1,)), ((), ())), preferred_element_type=f32)


def plan_blocks(tiles, count, bands, chunks):
    blocks = tiles.shape[0]
    index = jnp.arange(blocks, dtype=jnp.int32)
    band = jnp.where(index < count, tiles % bands, bands)
    same = band[:, None] == band[None, :]
    rank = jnp.sum((same & (index[None, :] < index[:, None])).astype(jnp.int32), axis=1)
    sizes = jnp.sum((band[None, :] == jnp.arange(bands, dtype=jnp.int32)[:, None]).astype(jnp.int32), axis=1)
    groups = (sizes + GROUP - 1) // GROUP
    upto = jnp.arange(bands)[None, :] <= jnp.arange(bands)[:, None]
    ends = jnp.sum(jnp.where(upto, groups[None, :], 0), axis=1)
    first = ends - groups
    mine = band[:, None] == jnp.arange(bands, dtype=jnp.int32)[None, :]
    slot = jnp.sum(jnp.where(mine, first[None, :] * GROUP, 0), axis=1) + rank
    slot = jnp.where(band < bands, slot, -1)
    spots = jnp.arange(chunks * GROUP, dtype=jnp.int32)
    code = index * 128 + tiles // bands
    spare = blocks * 128
    entries = spare + jnp.sum(jnp.where(slot[None, :] == spots[:, None], code[None, :] - spare, 0), axis=1)
    which = jnp.sum((jnp.arange(chunks)[:, None] >= ends[None, :]).astype(jnp.int32), axis=1)
    which = jnp.minimum(which, bands - 1)
    tail = jnp.stack([ends[-1], count])
    return entries.astype(jnp.int32), jnp.concatenate([which, tail]).astype(jnp.int32)


def misfit_kernel(
    entries, bands_of, image, cells, vis,
    near_re, near_im, turn_re, turn_im, span_re, span_im, swing_re, swing_im,
    wt_hi, wt_lo, wc_hi, wc_lo, rt_hi, rt_lo,
    y_hi, y_lo, hist, wg_hi, wg_lo, o_ref, r_ref,
):
    chunks = rt_hi.shape[0]
    bands = wc_hi.shape[0]
    side = image.shape[0]
    blocks = cells.shape[0]
    tall = wt_hi.shape[0]

    def build_rows(a, carry):
        pr = jnp.broadcast_to(turn_re[pl.ds(a, 1), :], (8, 128))
        pi = jnp.broadcast_to(turn_im[pl.ds(a, 1), :], (8, 128))
        for t in range(side // 128):
            at = slice(t * 128, (t + 1) * 128)
            nr, ni = near_re[:, at], near_im[:, at]
            both = jnp.concatenate([pr * nr - pi * ni, pr * ni + pi * nr], axis=0)
            high, low = split(both)
            wt_hi[a, :, at] = high
            wt_lo[a, :, at] = low
        return carry

    lax.fori_loop(0, tall, build_rows, 0, unroll=4)

    x_hi, x_lo = split(image[...])

    def build_cols(b, carry):
        cr = swing_re[b][None]
        ci = swing_im[b][None]
        sr = span_re[...].reshape(side // 8, 8, 128)
        si = span_im[...].reshape(side // 8, 8, 128)
        re = (cr * sr - ci * si).reshape(side, 128)
        im = (cr * si + ci * sr).reshape(side, 128)
        high, low = split(jnp.concatenate([re, im], axis=1))
        wc_hi[b] = high
        wc_lo[b] = low
        high, low = split(dot3(x_hi, x_lo, high, low))
        y_hi[b] = high
        y_lo[b] = low
        return carry

    lax.fori_loop(0, bands, build_cols, 0)

    hist[blocks] = jnp.zeros((24, 128), f32)
    rows8 = lax.broadcasted_iota(jnp.int32, (8, 128), 0)
    rows128 = lax.broadcasted_iota(jnp.int32, (128, 128), 0)

    def count_cells(g, carry):
        base = pl.multiple_of(g * GROUP, GROUP)
        q = cells[pl.ds(base, GROUP), :]
        qr = q // TILE_C
        qc = q - qr * TILE_C
        parts = []
        for p in range(2):
            v = vis[p, pl.ds(base, GROUP), :]
            high = v.astype(bf16).astype(f32)
            parts += [high, v - high]
        for s in range(GROUP):
            row = (rows8 == qr[s : s + 1]).astype(f32)
            pieces = [row] + [row * part[s : s + 1] for part in parts]
            lhs = jnp.concatenate(pieces + [jnp.zeros((8, 128), f32)], axis=0).astype(bf16)
            hot = (rows128 == qc[s : s + 1]).astype(f32).astype(bf16)
            out = nt(lhs, hot)
            hist[base + s, 0:8] = out[0:8]
            hist[base + s, 8:16] = out[8:16] + out[16:24]
            hist[base + s, 16:24] = out[24:32] + out[32:40]
        return carry

    lax.fori_loop(0, (bands_of[chunks + 1] + GROUP - 1) // GROUP, count_cells, 0)

    def work(c, carry):
        b = bands_of[c]
        for s in range(GROUP):
            a = entries[c * GROUP + s] & 127
            wg_hi[16 * s : 16 * s + 16] = wt_hi[a]
            wg_lo[16 * s : 16 * s + 16] = wt_lo[a]
        o_ref[...] = dot3(wg_hi[...], wg_lo[...], y_hi[b], y_lo[b])
        for s in range(GROUP):
            k = entries[c * GROUP + s] // 128
            top = slice(16 * s, 16 * s + 8)
            low = slice(16 * s + 8, 16 * s + 16)
            model_re = o_ref[top, 0:128] - o_ref[low, 128:256]
            model_im = o_ref[top, 128:256] + o_ref[low, 0:128]
            many = hist[k, 0:8]
            g_re = many * model_re - hist[k, 8:16]
            g_im = many * model_im - hist[k, 16:24]
            r_ref[top, 0:128] = g_re
            r_ref[top, 128:256] = g_im
            r_ref[low, 0:128] = g_im
            r_ref[low, 128:256] = -g_re
        high, low = split(r_ref[...].T)
        rt_hi[c] = high
        rt_lo[c] = low
        return carry

    lax.fori_loop(0, bands_of[chunks], work, 0)


def adjoint_kernel(entries, bands_of, rt_hi, rt_lo, wt_hi, wt_lo, wc_hi, wc_lo, out, z, wg_hi, wg_lo, acc):
    chunks = rt_hi.shape[0]
    bands = wc_hi.shape[0]
    z[...] = jnp.zeros_like(z)

    def gather(c, carry):
        b = bands_of[c]
        for s in range(GROUP):
            a = entries[c * GROUP + s] & 127
            wg_hi[16 * s : 16 * s + 16] = wt_hi[a]
            wg_lo[16 * s : 16 * s + 16] = wt_lo[a]
        z[b] += dot3(rt_hi[c], rt_lo[c], wg_hi[...], wg_lo[...])
        return carry

    lax.fori_loop(0, bands_of[chunks], gather, 0)
    acc[...] = jnp.zeros_like(acc)

    def back(b, carry):
        high, low = split(z[b])
        acc[...] += dot3(wc_hi[b], wc_lo[b], high, low)
        return carry

    lax.fori_loop(0, bands, back, 0)
    out[...] = acc[...].T


def whole(n):
    return [pl.BlockSpec(memory_space=pltpu.VMEM) for _ in range(n)]


def misfit_groups(plane, vis, cells, entries, bands_of):
    side = plane.shape[0]
    tables = [jnp.asarray(t) for t in small_tables(*plane.shape)]
    chunks = entries.shape[0] // GROUP
    bands = 2 * side // TILE_C
    tall = 2 * side // TILE_R
    blocks = cells.shape[0]
    shapes = [(tall, 16, side)] * 2 + [(bands, side, 256)] * 2 + [(chunks, 256, 256)] * 2
    return pl.pallas_call(
        misfit_kernel,
        out_shape=[jax.ShapeDtypeStruct(s, bf16) for s in shapes],
        grid_spec=pltpu.PrefetchScalarGridSpec(
            num_scalar_prefetch=2,
            grid=(),
            in_specs=whole(3 + len(tables)),
            out_specs=whole(6),
            scratch_shapes=[
                pltpu.VMEM((bands, side, 256), bf16),
                pltpu.VMEM((bands, side, 256), bf16),
                pltpu.VMEM((blocks + 1, 24, 128), f32),
                pltpu.VMEM((256, side), bf16),
                pltpu.VMEM((256, side), bf16),
                pltpu.VMEM((256, 256), f32),
                pltpu.VMEM((256, 256), f32),
            ],
        ),
        compiler_params=pltpu.CompilerParams(vmem_limit_bytes=VMEM_BYTES),
        name="misfit",
    )(entries, bands_of, plane, cells, vis, *tables)


def adjoint_image(entries, bands_of, rt_hi, rt_lo, wt_hi, wt_lo, wc_hi, wc_lo):
    bands, side, _ = wc_hi.shape
    return pl.pallas_call(
        adjoint_kernel,
        out_shape=jax.ShapeDtypeStruct((side, side), f32),
        grid_spec=pltpu.PrefetchScalarGridSpec(
            num_scalar_prefetch=2,
            grid=(),
            in_specs=whole(6),
            out_specs=whole(1)[0],
            scratch_shapes=[
                pltpu.VMEM((bands, 256, side), f32),
                pltpu.VMEM((256, side), bf16),
                pltpu.VMEM((256, side), bf16),
                pltpu.VMEM((side, side), f32),
            ],
        ),
        compiler_params=pltpu.CompilerParams(vmem_limit_bytes=VMEM_BYTES),
        name="adjoint",
    )(entries, bands_of, rt_hi, rt_lo, wt_hi, wt_lo, wc_hi, wc_lo)


def gram_kernel(dual, image, out):
    total = dual.shape[0]
    channels = out.shape[0]
    rows = total // channels
    high, low = split(dual[...] + sigma_step * image[...])
    full = nt(high, high) + nt(high, low) + nt(low, high)
    i = lax.broadcasted_iota(jnp.int32, (total, total), 0)
    j = lax.broadcasted_iota(jnp.int32, (total, total), 1)
    full = jnp.where(i % rows == j % rows, full, 0.0)
    ci = lax.broadcasted_iota(jnp.int32, (channels, total), 0)
    cj = lax.broadcasted_iota(jnp.int32, (channels, total), 1)
    pick = (cj // rows == ci).astype(f32).astype(bf16)

    def gather_left(x):
        a, rest = split(x)
        b, c = split(x - a.astype(f32))
        return sum(jnp.dot(pick, part, preferred_element_type=f32) for part in (a, b, c))

    half = gather_left(full)
    a, b = split(half)
    c = (half - a.astype(f32) - b.astype(f32)).astype(bf16)
    out[...] = nt(a, pick) + nt(b, pick) + nt(c, pick)


def lowrank_kernel(ridge, gram, dual, image, detail, lowrank, direction):
    total = dual.shape[0]
    channels = gram.shape[-1]
    rows = total // channels
    g = gram[0]
    for p in range(1, gram.shape[0]):
        g = g + gram[p]
    ci = lax.broadcasted_iota(jnp.int32, (channels, channels), 0)
    cj = lax.broadcasted_iota(jnp.int32, (channels, channels), 1)
    identity = (ci == cj).astype(f32)
    shifted = g + ridge * identity
    trace = jnp.sum(shifted * identity, keepdims=True)
    current = shifted / trace
    inverse = identity
    for turn in range(NS_STEPS):
        factor = 1.5 * identity - 0.5 * jnp.dot(inverse, current, precision=highest)
        current = jnp.dot(current, factor, precision=highest)
        inverse = jnp.dot(factor, inverse, precision=highest)
    root = inverse * (math.sqrt(ridge) * lax.rsqrt(trace))
    i = lax.broadcasted_iota(jnp.int32, (total, total), 0)
    j = lax.broadcasted_iota(jnp.int32, (total, total), 1)
    si = lax.broadcasted_iota(jnp.int32, (total, channels), 0)
    sj = lax.broadcasted_iota(jnp.int32, (total, channels), 1)
    pick = (si // rows == sj).astype(f32).astype(bf16)
    match = i % rows == j % rows

    def spread(x):
        wide = jnp.dot(pick, x, preferred_element_type=f32).astype(bf16)
        return jnp.where(match, nt(wide, pick), 0.0).astype(bf16)

    root_hi, root_lo = split(root)
    high, low = split(dual[...] + sigma_step * image[...])
    result = dot3(spread(root_hi), spread(root_lo), high, low)
    lowrank[...] = result
    direction[...] = 2.0 * result - dual[...] + detail[...]


def local_gram(dual, image, channels):
    return pl.pallas_call(
        gram_kernel,
        out_shape=jax.ShapeDtypeStruct((channels, channels), f32),
        in_specs=whole(2),
        out_specs=whole(1)[0],
        compiler_params=pltpu.CompilerParams(vmem_limit_bytes=VMEM_BYTES),
        name="gram",
    )(dual, image)


def lowrank_update(gram, dual, image, detail, ridge):
    return pl.pallas_call(
        functools.partial(lowrank_kernel, ridge),
        out_shape=[jax.ShapeDtypeStruct(dual.shape, f32)] * 2,
        in_specs=whole(4),
        out_specs=whole(2),
        compiler_params=pltpu.CompilerParams(vmem_limit_bytes=VMEM_BYTES),
        name="lowrank",
    )(gram, dual, image, detail)


def row_difference(rimmed):
    return rimmed[:, 1:-1] - 0.5 * (rimmed[:, :-2] + rimmed[:, 2:])


def column_difference(field):
    padded = jnp.pad(field, ((0, 0), (0, 0), (1, 1)))
    return padded[:, :, 1:-1] - 0.5 * (padded[:, :, :-2] + padded[:, :, 2:])


def neighbours(shard, width):
    devices = lax.axis_size(RING)
    up = [(i, i + 1) for i in range(devices - 1)]
    down = [(j, i) for i, j in up]
    return lax.ppermute(shard[:, -width:], RING, up), lax.ppermute(shard[:, :width], RING, down)


def per_device(
    image, visibilities, tile_index, cells, block_count, lowrank_dual, wavelet_dual, wavelet_bound
):
    side = image.shape[-1]
    channels, rows_here, _ = lowrank_dual.shape
    devices = lax.axis_size(RING)
    pieces = lax.axis_size("pix")
    here = lax.axis_index(RING)
    flat = (channels * rows_here, side)

    facet_image = lax.all_to_all(
        image.reshape(devices, rows_here, side), RING, split_axis=0, concat_axis=0, tiled=True
    )
    dual_before, dual_after = neighbours(wavelet_dual, 1)

    bands = 2 * side // TILE_C
    chunks = tile_index.shape[1] // GROUP + bands
    entries, bands_of = plan_blocks(tile_index[0], block_count[0], bands, chunks)
    groups = misfit_groups(image[0], visibilities[:, 0], cells[0], entries, bands_of)
    wt_hi, wt_lo, wc_hi, wc_lo, rt_hi, rt_lo = groups
    facet_image, rt_hi = lax.optimization_barrier((facet_image, rt_hi))

    image_before, image_after = neighbours(facet_image, 2)
    gram = local_gram(lowrank_dual.reshape(flat), facet_image.reshape(flat), channels)
    grams = [gram] + [
        lax.ppermute(gram, "pix", [(i, (i + s) % pieces) for i in range(pieces)]) for s in range(1, pieces)
    ]

    bound = wavelet_bound[:, None, None]
    rimmed = jnp.concatenate([image_before, facet_image, image_after], axis=1)
    dual_rimmed = jnp.concatenate([dual_before, wavelet_dual, dual_after], axis=1)
    next_rimmed = jnp.clip(
        dual_rimmed + sigma_step * column_difference(row_difference(rimmed)), -bound, bound
    )
    wavelet_next = next_rimmed[:, 1:-1]
    row = lax.broadcasted_iota(jnp.int32, (1, rows_here + 2, 1), 1) + here * rows_here
    inside = (row >= 1) & (row <= side)
    pushed = jnp.where(inside, 2.0 * next_rimmed - dual_rimmed, 0.0)
    back_detail = column_difference(row_difference(pushed))

    ridge = float(rows_here * side * pieces)
    lowrank_next, direction = lowrank_update(
        jnp.stack(grams),
        lowrank_dual.reshape(flat),
        facet_image.reshape(flat),
        back_detail.reshape(flat),
        ridge,
    )
    direction, rt_hi = lax.optimization_barrier((direction, rt_hi))
    returned = lax.all_to_all(
        direction.reshape(channels, rows_here, side), RING, split_axis=0, concat_axis=0, tiled=True
    )
    gradient = adjoint_image(entries, bands_of, rt_hi, rt_lo, wt_hi, wt_lo, wc_hi, wc_lo)
    returned = returned.reshape(side, side)
    image_next = jnp.maximum(image[0] - tau_step * (gradient + returned), 0.0)
    return (image_next[None], lowrank_next.reshape(lowrank_dual.shape), wavelet_next)


def solution(mesh):
    return jax.shard_map(
        per_device,
        mesh=mesh,
        in_specs=(
            P(RING, None, None),
            P(None, RING, None, None),
            P(RING, None),
            P(RING, None, None),
            P(RING),
            P(None, RING, None),
            P(None, RING, None),
            P(),
        ),
        out_specs=(P(RING, None, None), P(None, RING, None), P(None, RING, None)),
        check_vma=False,
    )
```

```python
import functools
import math

import jax
import jax.numpy as jnp
import numpy as np
from jax import lax
from jax.experimental import pallas as pl
from jax.experimental.pallas import tpu as pltpu
from jax.sharding import PartitionSpec as P

TILE_R = 8
TILE_C = 128
NS_STEPS = 5
GROUP = 16
PARTS = 4
RING = ("facet", "pix")

highest = lax.Precision.HIGHEST
tau_step = 0.5
sigma_step = 1.0
f32 = jnp.float32
bf16 = jnp.bfloat16
MIB = 1024 * 1024
BIG = 58 * MIB


def gauss(n):
    d = np.arange(n)[:, None] - np.arange(n)[None, :]
    return np.exp(-0.5 * d.astype(np.float64) ** 2)


def small_tables(height, width):
    rows, cols = 2 * height, 2 * width
    m = np.arange(height)
    n = np.arange(width)
    near = gauss(TILE_R) @ np.exp(-2j * np.pi * np.arange(TILE_R)[:, None] * m[None, :] / rows)
    period = rows // TILE_R
    turn = np.exp(
        -2j * np.pi * (np.arange(period)[:, None] * np.arange(period)[None, :] % period) / period
    )
    span = np.exp(-2j * np.pi * n[:, None] * np.arange(TILE_C)[None, :] / cols) @ gauss(TILE_C)
    span = span / height
    bands = cols // TILE_C
    swing = np.exp(-2j * np.pi * np.arange(bands)[:, None] * np.arange(8)[None, :] / bands)
    swing = np.broadcast_to(swing[:, :, None], (bands, 8, TILE_C))
    assert bands == 8 and period == 128
    near = near.reshape(TILE_R, -1, 128).transpose(1, 0, 2)
    parts = []
    for table in (span, swing, turn, near):
        parts += [table.real.reshape(-1, 128), table.imag.reshape(-1, 128)]
    return np.concatenate(parts).astype(np.float32), [len(part) for part in parts]


def table_views(table, sizes):
    views, start = [], 0
    for size in sizes:
        views.append(table.at[pl.ds(start, size)])
        start += size
    return views


def split(x):
    high = x.astype(bf16)
    return high, (x - high.astype(f32)).astype(bf16)


def dot3(a_hi, a_lo, b_hi, b_lo):
    return (
        jnp.dot(a_hi, b_hi, preferred_element_type=f32)
        + jnp.dot(a_lo, b_hi, preferred_element_type=f32)
        + jnp.dot(a_hi, b_lo, preferred_element_type=f32)
    )


def nt(a, b):
    return lax.dot_general(a, b, (((1,), (1,)), ((), ())), preferred_element_type=f32)


def plan_blocks(tiles, count, bands, chunks):
    blocks = tiles.shape[0]
    index = jnp.arange(blocks, dtype=jnp.int32)
    band = jnp.where(index < count, tiles % bands, bands)
    same = band[:, None] == band[None, :]
    rank = jnp.sum((same & (index[None, :] < index[:, None])).astype(jnp.int32), axis=1)
    sizes = jnp.sum((band[None, :] == jnp.arange(bands, dtype=jnp.int32)[:, None]).astype(jnp.int32), axis=1)
    groups = (sizes + GROUP - 1) // GROUP
    upto = jnp.arange(bands)[None, :] <= jnp.arange(bands)[:, None]
    ends = jnp.sum(jnp.where(upto, groups[None, :], 0), axis=1)
    first = ends - groups
    mine = band[:, None] == jnp.arange(bands, dtype=jnp.int32)[None, :]
    slot = jnp.sum(jnp.where(mine, first[None, :] * GROUP, 0), axis=1) + rank
    slot = jnp.where(band < bands, slot, -1)
    spots = jnp.arange(chunks * GROUP, dtype=jnp.int32)
    code = index * 128 + tiles // bands
    spare = blocks * 128
    entries = spare + jnp.sum(jnp.where(slot[None, :] == spots[:, None], code[None, :] - spare, 0), axis=1)
    which = jnp.sum((jnp.arange(chunks)[:, None] >= ends[None, :]).astype(jnp.int32), axis=1)
    which = jnp.minimum(which, bands - 1)
    return entries.astype(jnp.int32), jnp.concatenate([which, ends[-1:]]).astype(jnp.int32)


def column_band(b, span_re, span_im, swing_re, swing_im):
    side = span_re.shape[0]
    at = pl.ds(pl.multiple_of(b * 8, 8), 8)
    cr = swing_re[at][None]
    ci = swing_im[at][None]
    sr = span_re[...].reshape(side // 8, 8, TILE_C)
    si = span_im[...].reshape(side // 8, 8, TILE_C)
    re = (cr * sr - ci * si).reshape(side, TILE_C)
    im = (cr * si + ci * sr).reshape(side, TILE_C)
    return split(jnp.concatenate([re, im], axis=1))


def forward_kernel(
    sizes, live, image_in, cells_in, vis_in, table_in, y_out, hist_out,
    image, cells, vis, table, y, hist, x_hi, x_lo, in_sem, y_sem, hist_sem, spare_sem,
):
    bands = y.shape[1]
    blocks = cells.shape[0]
    reads = [
        pltpu.make_async_copy(source, to, in_sem.at[i])
        for i, (source, to) in enumerate(
            ((image_in, image), (table_in.at[pl.ds(0, table.shape[0])], table), (cells_in, cells), (vis_in, vis))
        )
    ]
    for read in reads:
        read.start()
    span_re, span_im, swing_re, swing_im = table_views(table, sizes)
    reads[0].wait()
    x_hi[...], x_lo[...] = split(image[...])
    reads[1].wait()

    def y_copy(part, b):
        return pltpu.make_async_copy(y.at[part, b], y_out.at[part, b], y_sem.at[part, b])

    def hist_copy(g):
        at = pl.ds(g * GROUP, GROUP)
        return pltpu.make_async_copy(hist.at[at], hist_out.at[at], hist_sem.at[g])

    def build_cols(b, carry):
        high, low = column_band(b, span_re, span_im, swing_re, swing_im)
        high, low = split(dot3(x_hi[...], x_lo[...], high, low))
        y[0, b] = high
        y[1, b] = low
        y_copy(0, b).start()
        y_copy(1, b).start()
        return carry

    lax.fori_loop(0, bands, build_cols, 0, unroll=2)

    reads[2].wait()
    reads[3].wait()
    hist[blocks] = jnp.zeros((24, 128), f32)
    spare = pltpu.make_async_copy(hist.at[pl.ds(blocks, 1)], hist_out.at[pl.ds(blocks, 1)], spare_sem)
    spare.start()
    rows8 = lax.broadcasted_iota(jnp.int32, (8, 128), 0)
    rows128 = lax.broadcasted_iota(jnp.int32, (128, 128), 0)

    def count_cells(g, carry):
        base = pl.multiple_of(g * GROUP, GROUP)
        q = cells[pl.ds(base, GROUP), :]
        qr = q // TILE_C
        qc = q - qr * TILE_C
        parts = []
        for p in range(2):
            v = vis[p, pl.ds(base, GROUP), :]
            high = v.astype(bf16).astype(f32)
            parts += [high, v - high]
        for s in range(GROUP):
            row = (rows8 == qr[s : s + 1]).astype(f32)
            pieces = [row] + [row * part[s : s + 1] for part in parts]
            lhs = jnp.concatenate(pieces + [jnp.zeros((8, 128), f32)], axis=0).astype(bf16)
            hot = (rows128 == qc[s : s + 1]).astype(f32).astype(bf16)
            out = nt(lhs, hot)
            hist[base + s, 0:8] = out[0:8]
            hist[base + s, 8:16] = out[8:16] + out[16:24]
            hist[base + s, 16:24] = out[24:32] + out[32:40]
        hist_copy(g).start()
        return carry

    groups = (live[0] + GROUP - 1) // GROUP
    lax.fori_loop(0, groups, count_cells, 0)

    def hist_wait(g, carry):
        hist_copy(g).wait()
        return carry

    lax.fori_loop(0, groups, hist_wait, 0)
    spare.wait()
    for part in range(2):
        for b in range(bands):
            y_copy(part, b).wait()


def adjoint_kernel(
    sizes, entries, bands_of, image_in, y_in, hist_in, table_in,
    out, image, y, hist, table, sems, wt_hi, wt_lo, z, acc, r_ref, *sets,
):
    side = image.shape[0]
    bands = y.shape[1]
    chunks = entries.shape[0] // GROUP
    reads = [
        pltpu.make_async_copy(source, to, sems.at[i])
        for i, (source, to) in enumerate(((table_in, table), (y_in, y), (hist_in, hist), (image_in, image)))
    ]
    for read in reads:
        read.start()
    span_re, span_im, swing_re, swing_im, turn_re, turn_im, near_re, near_im = table_views(table, sizes)
    reads[0].wait()
    tall = wt_hi.shape[0]
    sets = (sets[:3], sets[3:])

    def build_rows(a, carry):
        pr = jnp.broadcast_to(turn_re[pl.ds(a, 1), :], (8, 128))
        pi = jnp.broadcast_to(turn_im[pl.ds(a, 1), :], (8, 128))
        for t in range(side // 128):
            at = slice(t * 128, (t + 1) * 128)
            nr, ni = near_re[8 * t : 8 * t + 8], near_im[8 * t : 8 * t + 8]
            both = jnp.concatenate([pr * nr - pi * ni, pr * ni + pi * nr], axis=0)
            high, low = split(both)
            wt_hi[a, :, at] = high
            wt_lo[a, :, at] = low
        return carry

    lax.fori_loop(0, tall, build_rows, 0, unroll=4)
    z[...] = jnp.zeros_like(z)
    for read in reads[1:]:
        read.wait()

    def evaluate(c, refs):
        wg_hi, wg_lo, o_ref = refs
        b = bands_of[c]
        for s in range(GROUP):
            a = entries[c * GROUP + s] & 127
            wg_hi[16 * s : 16 * s + 16] = wt_hi[a]
            wg_lo[16 * s : 16 * s + 16] = wt_lo[a]
        o_ref[...] = dot3(wg_hi[...], wg_lo[...], y[0, b], y[1, b])

    def spread(c, refs):
        wg_hi, wg_lo, o_ref = refs
        for s in range(GROUP):
            k = entries[c * GROUP + s] // 128
            top = slice(16 * s, 16 * s + 8)
            low = slice(16 * s + 8, 16 * s + 16)
            model_re = o_ref[top, 0:128] - o_ref[low, 128:256]
            model_im = o_ref[top, 128:256] + o_ref[low, 0:128]
            many = hist[k, 0:8]
            g_re = many * model_re - hist[k, 8:16]
            g_im = many * model_im - hist[k, 16:24]
            r_ref[top, 0:128] = g_re
            r_ref[top, 128:256] = g_im
            r_ref[low, 0:128] = g_im
            r_ref[low, 128:256] = -g_re
        rt_hi, rt_lo = split(r_ref[...].T)
        z[bands_of[c]] += dot3(rt_hi, rt_lo, wg_hi[...], wg_lo[...])

    evaluate(0, sets[0])

    def work(i, carry):
        evaluate(2 * i + 1, sets[1])
        spread(2 * i, sets[0])
        evaluate(2 * i + 2, sets[0])
        spread(2 * i + 1, sets[1])
        return carry

    lax.fori_loop(0, (bands_of[chunks] + 1) // 2, work, 0)
    acc[...] = jnp.zeros_like(acc)

    def back(b, carry):
        wc_hi, wc_lo = column_band(b, span_re, span_im, swing_re, swing_im)
        high, low = split(z[b])
        acc[...] += dot3(wc_hi, wc_lo, high, low)
        return carry

    lax.fori_loop(0, bands, back, 0, unroll=2)
    out[...] = image[...] - tau_step * acc[...].T


def whole(n):
    return [pl.BlockSpec(memory_space=pltpu.VMEM) for _ in range(n)]


def in_hbm(n):
    return [pl.BlockSpec(memory_space=pltpu.HBM) for _ in range(n)]


def forward(plane, vis, cells, count, table, sizes):
    side = plane.shape[0]
    bands = 2 * side // TILE_C
    blocks = cells.shape[0]
    y = (2, bands, side, 256)
    hist = (blocks + 1, 24, 128)
    return pl.pallas_call(
        functools.partial(forward_kernel, sizes[:4]),
        out_shape=[jax.ShapeDtypeStruct(y, bf16), jax.ShapeDtypeStruct(hist, f32)],
        grid_spec=pltpu.PrefetchScalarGridSpec(
            num_scalar_prefetch=1,
            grid=(),
            in_specs=in_hbm(4),
            out_specs=in_hbm(2),
            scratch_shapes=[
                pltpu.VMEM(plane.shape, f32),
                pltpu.VMEM(cells.shape, jnp.int32),
                pltpu.VMEM(vis.shape, f32),
                pltpu.VMEM((sum(sizes[:4]), 128), f32),
                pltpu.VMEM(y, bf16),
                pltpu.VMEM(hist, f32),
                pltpu.VMEM((side, side), bf16),
                pltpu.VMEM((side, side), bf16),
                pltpu.SemaphoreType.DMA((4,)),
                pltpu.SemaphoreType.DMA((2, bands)),
                pltpu.SemaphoreType.DMA((blocks // GROUP,)),
                pltpu.SemaphoreType.DMA,
            ],
        ),
        compiler_params=pltpu.CompilerParams(vmem_limit_bytes=BIG),
        name="forward",
    )(count, plane, cells, vis, table)


def adjoint(entries, bands_of, plane, y, hist, table, sizes):
    _, bands, side, _ = y.shape
    tall = 2 * side // TILE_R
    buffers = [pltpu.VMEM((256, side), bf16), pltpu.VMEM((256, side), bf16), pltpu.VMEM((256, 256), f32)]
    return pl.pallas_call(
        functools.partial(adjoint_kernel, sizes),
        out_shape=jax.ShapeDtypeStruct((side, side), f32),
        grid_spec=pltpu.PrefetchScalarGridSpec(
            num_scalar_prefetch=2,
            grid=(),
            in_specs=in_hbm(4),
            out_specs=whole(1)[0],
            scratch_shapes=[
                pltpu.VMEM(plane.shape, f32),
                pltpu.VMEM(y.shape, bf16),
                pltpu.VMEM(hist.shape, f32),
                pltpu.VMEM(table.shape, f32),
                pltpu.SemaphoreType.DMA((4,)),
                pltpu.VMEM((tall, 16, side), bf16),
                pltpu.VMEM((tall, 16, side), bf16),
                pltpu.VMEM((bands, 256, side), f32),
                pltpu.VMEM((side, side), f32),
                pltpu.VMEM((256, 256), f32),
            ]
            + buffers * 2,
        ),
        compiler_params=pltpu.CompilerParams(vmem_limit_bytes=BIG),
        name="adjoint",
    )(entries, bands_of, plane, y, hist, table)


def halo_kernel(image, edge_rows, up, down):
    channels = up.shape[1]
    rows = image.shape[0] // channels
    for c in range(channels):
        for i in range(2):
            up[i, c : c + 1] = image[(c + 1) * rows - 2 + i : (c + 1) * rows - 1 + i]
            down[i, c : c + 1] = image[c * rows + i : c * rows + i + 1]
    up[2] = edge_rows[1]
    down[2] = edge_rows[0]


def gram_kernel(dual, image, out):
    pick, match = row_maps(dual.shape[0], out.shape[0])
    high, low = split(dual[...] + sigma_step * image[...])
    full = jnp.where(match, nt(high, high) + nt(high, low) + nt(low, high), 0.0)

    def three(x):
        a, rest = split(x)
        b, c = split(x - a.astype(f32))
        return a, b, c

    half = sum(
        lax.dot_general(pick, part, (((0,), (0,)), ((), ())), preferred_element_type=f32)
        for part in three(full)
    )
    out[...] = sum(jnp.dot(part, pick, preferred_element_type=f32) for part in three(half))


def inverse_root(gram, ridge):
    channels = gram.shape[0]
    ci = lax.broadcasted_iota(jnp.int32, (channels, channels), 0)
    cj = lax.broadcasted_iota(jnp.int32, (channels, channels), 1)
    identity = (ci == cj).astype(f32)
    shifted = gram + ridge * identity
    trace = jnp.sum(shifted * identity, keepdims=True)
    current = shifted / trace
    factor = 1.5 * identity - 0.5 * current
    inverse = factor
    for turn in range(1, NS_STEPS):
        current = jnp.dot(current, factor, precision=highest)
        factor = 1.5 * identity - 0.5 * jnp.dot(inverse, current, precision=highest)
        inverse = jnp.dot(factor, inverse, precision=highest)
    return inverse * (math.sqrt(ridge) * lax.rsqrt(trace))


def dual_kernel(ridge, bound, edges, *refs):
    *grams, limit, image, flat_image, up, down = refs[:-19]
    before_in, after_in, dual_in, low_in, wavelet_out, lowrank_out, direction_out = refs[-19:-12]
    before, after, dual, low, wavelet, lowrank, direction, b_hi, b_lo, rims, in_sem, out_sem = refs[-12:]
    reads = [
        pltpu.make_async_copy(source, to, in_sem.at[i])
        for i, (source, to) in enumerate(((low_in, low), (before_in, before), (after_in, after), (dual_in, dual)))
    ]
    for read in reads:
        read.start()
    channels, rows, side = image.shape
    total = channels * rows
    gram = grams[0][...]
    for other in grams[1:]:
        gram = gram + other[...]
    root_hi, root_lo = split(inverse_root(gram, ridge))
    for read in reads:
        read.wait()
    b_hi[...], b_lo[...] = split(low[...] + sigma_step * flat_image[...])
    most = limit[...]

    def rim(middle, inner, outer, held, inside):
        step = columns(middle - 0.5 * (inner + outer))
        return inside * (2.0 * jnp.clip(held + sigma_step * step, -most, most) - held)

    rims[0] = rim(before[1], down[0], before[0], before[2], edges[0])
    rims[1] = rim(after[0], up[1], after[1], after[2], edges[1])
    step_rows = total // PARTS
    step_channels = channels // PARTS
    other, match = row_maps(total, channels)
    match = match[:step_rows]

    def copies(part):
        at = pl.ds(part * step_channels, step_channels)
        pairs = ((direction, direction_out), (wavelet, wavelet_out), (lowrank, lowrank_out))
        return [pltpu.make_async_copy(f.at[at], t.at[at], out_sem.at[i, part]) for i, (f, t) in enumerate(pairs)]

    def one(part, carry):
        pick, _ = row_maps(total, channels, part * step_rows, step_rows)

        def spread(x):
            wide = jnp.dot(pick, x, preferred_element_type=f32).astype(bf16)
            return jnp.where(match, nt(wide, other), 0.0).astype(bf16)

        result = dot3(spread(root_hi), spread(root_lo), b_hi[...], b_lo[...])
        held = low[pl.ds(pl.multiple_of(part * step_rows, step_rows), step_rows), :]
        part_sum = tau_step * (2.0 * result - held)
        for i in range(step_channels):
            c = part * step_channels + i
            at = pl.ds(c, 1)
            w = dual[c]
            b = bound[c]
            step = columns(rows_between(image[c], before[1, at], after[0, at]))
            new = jnp.clip(w + sigma_step * step, -b, b)
            wavelet[c] = new
            detail = columns(rows_between(2.0 * new - w, rims[0, at], rims[1, at]))
            mine = slice(i * rows, (i + 1) * rows)
            lowrank[c] = result[mine]
            direction[c] = part_sum[mine] + tau_step * detail
        for copy in copies(part):
            copy.start()
        return carry

    lax.fori_loop(0, PARTS, one, 0)
    for part in range(PARTS):
        for copy in copies(part):
            copy.wait()


def shift_lanes(x):
    wide = x.shape[-1]
    lane = lax.broadcasted_iota(jnp.int32, x.shape, 1)
    before = jnp.where(lane == 0, 0.0, pltpu.roll(x, 1, 1))
    after = jnp.where(lane == wide - 1, 0.0, pltpu.roll(x, wide - 1, 1))
    return before + after


def columns(x):
    return x - 0.5 * shift_lanes(x)


def rows_between(x, above, below):
    height = x.shape[0]
    row = lax.broadcasted_iota(jnp.int32, x.shape, 0)
    up = jnp.where(row == 0, above, pltpu.roll(x, 1, 0))
    down = jnp.where(row == height - 1, below, pltpu.roll(x, height - 1, 0))
    return x - 0.5 * (up + down)


def row_maps(total, channels, start=0, count=None):
    rows = total // channels
    count = total if count is None else count
    si = lax.broadcasted_iota(jnp.int32, (count, channels), 0) + start
    sj = lax.broadcasted_iota(jnp.int32, (count, channels), 1)
    pick = ((si >= sj * rows) & (si < sj * rows + rows)).astype(f32).astype(bf16)
    i = lax.rem(lax.broadcasted_iota(jnp.int32, (count, 1), 0), rows)
    j = lax.rem(lax.broadcasted_iota(jnp.int32, (1, total), 1), rows)
    return pick, i == j


def halo_rows(image, edge_rows):
    halo = jax.ShapeDtypeStruct((3,) + edge_rows.shape[1:], f32)
    return pl.pallas_call(
        halo_kernel,
        out_shape=[halo, halo],
        in_specs=whole(2),
        out_specs=whole(2),
        compiler_params=pltpu.CompilerParams(vmem_limit_bytes=8 * MIB),
        name="halo",
    )(image, edge_rows)


def local_gram(dual, image, channels):
    return pl.pallas_call(
        gram_kernel,
        out_shape=jax.ShapeDtypeStruct((channels, channels), f32),
        in_specs=whole(2),
        out_specs=whole(1)[0],
        compiler_params=pltpu.CompilerParams(vmem_limit_bytes=12 * MIB),
        name="gram",
    )(dual, image)


def final_kernel(base_in, sent_in, out_ref, base, sent, out, in_sem, out_sem):
    step = base.shape[0] // PARTS

    def reads(part):
        at = pl.ds(part * step, step)
        return [
            pltpu.make_async_copy(f.at[at], t.at[at], in_sem.at[i, part])
            for i, (f, t) in enumerate(((base_in, base), (sent_in, sent)))
        ]

    def write(part):
        at = pl.ds(part * step, step)
        return pltpu.make_async_copy(out.at[at], out_ref.at[at], out_sem.at[part])

    for part in range(PARTS):
        for read in reads(part):
            read.start()
    for part in range(PARTS):
        for read in reads(part):
            read.wait()
        at = slice(part * step, (part + 1) * step)
        out[at] = jnp.maximum(base[at] - sent[at], 0.0)
        write(part).start()
    for part in range(PARTS):
        write(part).wait()


def final_image(base, sent):
    return pl.pallas_call(
        final_kernel,
        out_shape=jax.ShapeDtypeStruct(base.shape, f32),
        in_specs=in_hbm(2),
        out_specs=in_hbm(1)[0],
        scratch_shapes=[pltpu.VMEM(base.shape, f32)] * 3
        + [pltpu.SemaphoreType.DMA((2, PARTS)), pltpu.SemaphoreType.DMA((PARTS,))],
        compiler_params=pltpu.CompilerParams(vmem_limit_bytes=8 * MIB),
        name="final",
    )(base, sent)


def dual_update(ridge, bound, edges, grams, image, up, down, before, after, dual, low):
    channels, rows, side = image.shape
    flat = (channels * rows, side)
    smem = pl.BlockSpec(memory_space=pltpu.SMEM)
    return pl.pallas_call(
        functools.partial(dual_kernel, ridge),
        out_shape=[jax.ShapeDtypeStruct(image.shape, f32)] * 3,
        in_specs=[smem, smem] + whole(len(grams) + 5) + in_hbm(4),
        out_specs=in_hbm(3),
        scratch_shapes=[
            pltpu.VMEM(before.shape, f32),
            pltpu.VMEM(after.shape, f32),
            pltpu.VMEM(image.shape, f32),
            pltpu.VMEM(flat, f32),
            pltpu.VMEM(image.shape, f32),
            pltpu.VMEM(image.shape, f32),
            pltpu.VMEM(image.shape, f32),
            pltpu.VMEM(flat, bf16),
            pltpu.VMEM(flat, bf16),
            pltpu.VMEM((2, channels, side), f32),
            pltpu.SemaphoreType.DMA((4,)),
            pltpu.SemaphoreType.DMA((3, PARTS)),
        ],
        compiler_params=pltpu.CompilerParams(vmem_limit_bytes=24 * MIB),
        name="dual",
    )(bound, edges, *grams, bound[:, None], image, image.reshape(flat), up, down, before, after, dual, low.reshape(flat))


def per_device(
    image, visibilities, tile_index, cells, block_count, lowrank_dual, wavelet_dual, wavelet_bound
):
    side = image.shape[-1]
    channels, rows_here, _ = lowrank_dual.shape
    devices = lax.axis_size(RING)
    pieces = lax.axis_size("pix")
    here = lax.axis_index(RING)
    flat = (channels * rows_here, side)

    facet_image = lax.all_to_all(
        image.reshape(devices, rows_here, side), RING, split_axis=0, concat_axis=0, tiled=True
    )

    bands = 2 * side // TILE_C
    chunks = tile_index.shape[1] // GROUP + bands + 1
    table, sizes = small_tables(side, side)
    table = jnp.asarray(table)
    entries, bands_of = plan_blocks(tile_index[0], block_count[0], bands, chunks)
    y, hist = forward(image[0], visibilities[:, 0], cells[0], block_count, table, sizes)
    edge_rows = jnp.stack([wavelet_dual[:, 0], wavelet_dual[:, -1]])
    edges = jnp.stack([here > 0, here < devices - 1]).astype(f32)
    facet_image, y, entries, bands_of, edge_rows, edges = lax.optimization_barrier(
        (facet_image, y, entries, bands_of, edge_rows, edges)
    )

    up, down = halo_rows(facet_image.reshape(flat), edge_rows)
    ahead = [(i, i + 1) for i in range(devices - 1)]
    before = lax.ppermute(up, RING, ahead)
    after = lax.ppermute(down, RING, [(j, i) for i, j in ahead])
    gram = local_gram(lowrank_dual.reshape(flat), facet_image.reshape(flat), channels)
    grams = [gram] + [
        lax.ppermute(gram, "pix", [(i, (i + s) % pieces) for i in range(pieces)]) for s in range(1, pieces)
    ]
    ridge = float(rows_here * side * pieces)
    wavelet_next, lowrank_next, direction = dual_update(
        ridge, wavelet_bound, edges, grams, facet_image, up, down, before, after, wavelet_dual, lowrank_dual
    )
    direction, y = lax.optimization_barrier((direction, y))
    returned = lax.all_to_all(direction, RING, split_axis=0, concat_axis=0, tiled=True)
    base = adjoint(entries, bands_of, image[0], y, hist, table, sizes)
    image_next = final_image(base, returned.reshape(side, side))
    return (image_next[None], lowrank_next, wavelet_next)


def solution(mesh):
    return jax.shard_map(
        per_device,
        mesh=mesh,
        in_specs=(
            P(RING, None, None),
            P(None, RING, None, None),
            P(RING, None),
            P(RING, None, None),
            P(RING),
            P(None, RING, None),
            P(None, RING, None),
            P(),
        ),
        out_specs=(P(RING, None, None), P(None, RING, None), P(None, RING, None)),
        check_vma=False,
    )
```

```python
import functools
import math

import jax
import jax.numpy as jnp
import numpy as np
from jax import lax
from jax.experimental import pallas as pl
from jax.experimental.pallas import tpu as pltpu
from jax.sharding import PartitionSpec as P

TILE_R = 8
TILE_C = 128
NS_STEPS = 5
GROUP = 16
PARTS = 4
HALVES = 1
RING = ("facet", "pix")

highest = lax.Precision.HIGHEST
tau_step = 0.5
sigma_step = 1.0
f32 = jnp.float32
bf16 = jnp.bfloat16
MIB = 1024 * 1024
BIG = 58 * MIB


def gauss(n):
    d = np.arange(n)[:, None] - np.arange(n)[None, :]
    return np.exp(-0.5 * d.astype(np.float64) ** 2)


def small_tables(height, width):
    rows, cols = 2 * height, 2 * width
    m = np.arange(height)
    n = np.arange(width)
    near = gauss(TILE_R) @ np.exp(-2j * np.pi * np.arange(TILE_R)[:, None] * m[None, :] / rows)
    period = rows // TILE_R
    turn = np.exp(
        -2j * np.pi * (np.arange(period)[:, None] * np.arange(period)[None, :] % period) / period
    )
    span = np.exp(-2j * np.pi * n[:, None] * np.arange(TILE_C)[None, :] / cols) @ gauss(TILE_C)
    span = span / height
    bands = cols // TILE_C
    swing = np.exp(-2j * np.pi * np.arange(bands)[:, None] * np.arange(8)[None, :] / bands)
    swing = np.broadcast_to(swing[:, :, None], (bands, 8, TILE_C))
    assert bands == 8 and period == 128
    near = near.reshape(TILE_R, -1, 128).transpose(1, 0, 2)
    parts = []
    for table in (span, swing, turn, near):
        parts += [table.real.reshape(-1, 128), table.imag.reshape(-1, 128)]
    return np.concatenate(parts).astype(np.float32), [len(part) for part in parts]


def table_views(table, sizes):
    views, start = [], 0
    for size in sizes:
        views.append(table.at[pl.ds(start, size)])
        start += size
    return views


def split(x):
    high = x.astype(bf16)
    return high, (x - high.astype(f32)).astype(bf16)


def dot3(a_hi, a_lo, b_hi, b_lo):
    return (
        jnp.dot(a_hi, b_hi, preferred_element_type=f32)
        + jnp.dot(a_lo, b_hi, preferred_element_type=f32)
        + jnp.dot(a_hi, b_lo, preferred_element_type=f32)
    )


def nt(a, b):
    return lax.dot_general(a, b, (((1,), (1,)), ((), ())), preferred_element_type=f32)


def plan_blocks(tiles, count, bands, chunks):
    blocks = tiles.shape[0]
    index = jnp.arange(blocks, dtype=jnp.int32)
    band = jnp.where(index < count, tiles % bands, bands)
    same = band[:, None] == band[None, :]
    rank = jnp.sum((same & (index[None, :] < index[:, None])).astype(jnp.int32), axis=1)
    sizes = jnp.sum((band[None, :] == jnp.arange(bands, dtype=jnp.int32)[:, None]).astype(jnp.int32), axis=1)
    groups = (sizes + GROUP - 1) // GROUP
    upto = jnp.arange(bands)[None, :] <= jnp.arange(bands)[:, None]
    ends = jnp.sum(jnp.where(upto, groups[None, :], 0), axis=1)
    first = ends - groups
    mine = band[:, None] == jnp.arange(bands, dtype=jnp.int32)[None, :]
    slot = jnp.sum(jnp.where(mine, first[None, :] * GROUP, 0), axis=1) + rank
    slot = jnp.where(band < bands, slot, -1)
    spots = jnp.arange(chunks * GROUP, dtype=jnp.int32)
    code = index * 128 + tiles // bands
    spare = blocks * 128
    entries = spare + jnp.sum(jnp.where(slot[None, :] == spots[:, None], code[None, :] - spare, 0), axis=1)
    which = jnp.sum((jnp.arange(chunks)[:, None] >= ends[None, :]).astype(jnp.int32), axis=1)
    which = jnp.minimum(which, bands - 1)
    return entries.astype(jnp.int32), jnp.concatenate([which, ends[-1:]]).astype(jnp.int32)


def column_band(b, span_re, span_im, swing_re, swing_im):
    side = span_re.shape[0]
    at = pl.ds(pl.multiple_of(b * 8, 8), 8)
    cr = swing_re[at][None]
    ci = swing_im[at][None]
    sr = span_re[...].reshape(side // 8, 8, TILE_C)
    si = span_im[...].reshape(side // 8, 8, TILE_C)
    re = (cr * sr - ci * si).reshape(side, TILE_C)
    im = (cr * si + ci * sr).reshape(side, TILE_C)
    return split(jnp.concatenate([re, im], axis=1))


def forward_kernel(
    sizes, live, image_in, cells_in, vis_in, table_in, y_out, hist_out,
    image, cells, vis, table, y, hist, x_hi, x_lo, in_sem, y_sem, hist_sem, spare_sem,
):
    bands = y.shape[1]
    blocks = cells.shape[0]
    reads = [
        pltpu.make_async_copy(source, to, in_sem.at[i])
        for i, (source, to) in enumerate(
            ((image_in, image), (table_in.at[pl.ds(0, table.shape[0])], table), (cells_in, cells), (vis_in, vis))
        )
    ]
    for read in reads:
        read.start()
    span_re, span_im, swing_re, swing_im = table_views(table, sizes)
    reads[0].wait()
    x_hi[...], x_lo[...] = split(image[...])
    reads[1].wait()

    def y_copy(part, b):
        return pltpu.make_async_copy(y.at[part, b], y_out.at[part, b], y_sem.at[part, b])

    def hist_copy(g):
        at = pl.ds(g * GROUP, GROUP)
        return pltpu.make_async_copy(hist.at[at], hist_out.at[at], hist_sem.at[g])

    def build_cols(b, carry):
        high, low = column_band(b, span_re, span_im, swing_re, swing_im)
        high, low = split(dot3(x_hi[...], x_lo[...], high, low))
        y[0, b] = high
        y[1, b] = low
        y_copy(0, b).start()
        y_copy(1, b).start()
        return carry

    lax.fori_loop(0, bands, build_cols, 0, unroll=2)

    reads[2].wait()
    reads[3].wait()
    hist[blocks] = jnp.zeros((24, 128), f32)
    spare = pltpu.make_async_copy(hist.at[pl.ds(blocks, 1)], hist_out.at[pl.ds(blocks, 1)], spare_sem)
    spare.start()
    rows8 = lax.broadcasted_iota(jnp.int32, (8, 128), 0)
    rows128 = lax.broadcasted_iota(jnp.int32, (128, 128), 0)

    def count_cells(g, carry):
        base = pl.multiple_of(g * GROUP, GROUP)
        q = cells[pl.ds(base, GROUP), :]
        qr = q // TILE_C
        qc = q - qr * TILE_C
        parts = []
        for p in range(2):
            v = vis[p, pl.ds(base, GROUP), :]
            high = v.astype(bf16).astype(f32)
            parts += [high, v - high]
        for s in range(GROUP):
            row = (rows8 == qr[s : s + 1]).astype(f32)
            pieces = [row] + [row * part[s : s + 1] for part in parts]
            lhs = jnp.concatenate(pieces + [jnp.zeros((8, 128), f32)], axis=0).astype(bf16)
            hot = (rows128 == qc[s : s + 1]).astype(f32).astype(bf16)
            out = nt(lhs, hot)
            hist[base + s, 0:8] = out[0:8]
            hist[base + s, 8:16] = out[8:16] + out[16:24]
            hist[base + s, 16:24] = out[24:32] + out[32:40]
        hist_copy(g).start()
        return carry

    groups = (live[0] + GROUP - 1) // GROUP
    lax.fori_loop(0, groups, count_cells, 0)

    def hist_wait(g, carry):
        hist_copy(g).wait()
        return carry

    lax.fori_loop(0, groups, hist_wait, 0)
    spare.wait()
    for part in range(2):
        for b in range(bands):
            y_copy(part, b).wait()


def adjoint_kernel(
    sizes, entries, bands_of, image_in, y_in, hist_in, table_in,
    out, image, y, hist, table, sems, wt_hi, wt_lo, z, acc, r_ref, *sets,
):
    side = image.shape[0]
    bands = y.shape[1]
    chunks = entries.shape[0] // GROUP
    reads = [
        pltpu.make_async_copy(source, to, sems.at[i])
        for i, (source, to) in enumerate(((table_in, table), (y_in, y), (hist_in, hist), (image_in, image)))
    ]
    for read in reads:
        read.start()
    span_re, span_im, swing_re, swing_im, turn_re, turn_im, near_re, near_im = table_views(table, sizes)
    reads[0].wait()
    tall = wt_hi.shape[0]
    sets = (sets[:3], sets[3:])

    def build_rows(a, carry):
        pr = jnp.broadcast_to(turn_re[pl.ds(a, 1), :], (8, 128))
        pi = jnp.broadcast_to(turn_im[pl.ds(a, 1), :], (8, 128))
        for t in range(side // 128):
            at = slice(t * 128, (t + 1) * 128)
            nr, ni = near_re[8 * t : 8 * t + 8], near_im[8 * t : 8 * t + 8]
            both = jnp.concatenate([pr * nr - pi * ni, pr * ni + pi * nr], axis=0)
            high, low = split(both)
            wt_hi[a, :, at] = high
            wt_lo[a, :, at] = low
        return carry

    lax.fori_loop(0, tall, build_rows, 0, unroll=4)
    z[...] = jnp.zeros_like(z)
    for read in reads[1:]:
        read.wait()

    def evaluate(c, refs):
        wg_hi, wg_lo, o_ref = refs
        b = bands_of[c]
        for s in range(GROUP):
            a = entries[c * GROUP + s] & 127
            wg_hi[16 * s : 16 * s + 16] = wt_hi[a]
            wg_lo[16 * s : 16 * s + 16] = wt_lo[a]
        o_ref[...] = dot3(wg_hi[...], wg_lo[...], y[0, b], y[1, b])

    def spread(c, refs):
        wg_hi, wg_lo, o_ref = refs
        for s in range(GROUP):
            k = entries[c * GROUP + s] // 128
            top = slice(16 * s, 16 * s + 8)
            low = slice(16 * s + 8, 16 * s + 16)
            model_re = o_ref[top, 0:128] - o_ref[low, 128:256]
            model_im = o_ref[top, 128:256] + o_ref[low, 0:128]
            many = hist[k, 0:8]
            g_re = many * model_re - hist[k, 8:16]
            g_im = many * model_im - hist[k, 16:24]
            r_ref[top, 0:128] = g_re
            r_ref[top, 128:256] = g_im
            r_ref[low, 0:128] = g_im
            r_ref[low, 128:256] = -g_re
        rt_hi, rt_lo = split(r_ref[...].T)
        z[bands_of[c]] += dot3(rt_hi, rt_lo, wg_hi[...], wg_lo[...])

    evaluate(0, sets[0])

    def work(i, carry):
        evaluate(2 * i + 1, sets[1])
        spread(2 * i, sets[0])
        evaluate(2 * i + 2, sets[0])
        spread(2 * i + 1, sets[1])
        return carry

    lax.fori_loop(0, (bands_of[chunks] + 1) // 2, work, 0)
    acc[...] = jnp.zeros_like(acc)

    def back(b, carry):
        wc_hi, wc_lo = column_band(b, span_re, span_im, swing_re, swing_im)
        high, low = split(z[b])
        acc[...] += dot3(wc_hi, wc_lo, high, low)
        return carry

    lax.fori_loop(0, bands, back, 0, unroll=2)
    out[...] = image[...] - tau_step * acc[...].T


def whole(n):
    return [pl.BlockSpec(memory_space=pltpu.VMEM) for _ in range(n)]


def in_hbm(n):
    return [pl.BlockSpec(memory_space=pltpu.HBM) for _ in range(n)]


def forward(plane, vis, cells, count, table, sizes):
    side = plane.shape[0]
    bands = 2 * side // TILE_C
    blocks = cells.shape[0]
    y = (2, bands, side, 256)
    hist = (blocks + 1, 24, 128)
    return pl.pallas_call(
        functools.partial(forward_kernel, sizes[:4]),
        out_shape=[jax.ShapeDtypeStruct(y, bf16), jax.ShapeDtypeStruct(hist, f32)],
        grid_spec=pltpu.PrefetchScalarGridSpec(
            num_scalar_prefetch=1,
            grid=(),
            in_specs=in_hbm(4),
            out_specs=in_hbm(2),
            scratch_shapes=[
                pltpu.VMEM(plane.shape, f32),
                pltpu.VMEM(cells.shape, jnp.int32),
                pltpu.VMEM(vis.shape, f32),
                pltpu.VMEM((sum(sizes[:4]), 128), f32),
                pltpu.VMEM(y, bf16),
                pltpu.VMEM(hist, f32),
                pltpu.VMEM((side, side), bf16),
                pltpu.VMEM((side, side), bf16),
                pltpu.SemaphoreType.DMA((4,)),
                pltpu.SemaphoreType.DMA((2, bands)),
                pltpu.SemaphoreType.DMA((blocks // GROUP,)),
                pltpu.SemaphoreType.DMA,
            ],
        ),
        compiler_params=pltpu.CompilerParams(vmem_limit_bytes=BIG),
        name="forward",
    )(count, plane, cells, vis, table)


def adjoint(entries, bands_of, plane, y, hist, table, sizes):
    _, bands, side, _ = y.shape
    tall = 2 * side // TILE_R
    buffers = [pltpu.VMEM((256, side), bf16), pltpu.VMEM((256, side), bf16), pltpu.VMEM((256, 256), f32)]
    return pl.pallas_call(
        functools.partial(adjoint_kernel, sizes),
        out_shape=jax.ShapeDtypeStruct((side, side), f32),
        grid_spec=pltpu.PrefetchScalarGridSpec(
            num_scalar_prefetch=2,
            grid=(),
            in_specs=in_hbm(4),
            out_specs=whole(1)[0],
            scratch_shapes=[
                pltpu.VMEM(plane.shape, f32),
                pltpu.VMEM(y.shape, bf16),
                pltpu.VMEM(hist.shape, f32),
                pltpu.VMEM(table.shape, f32),
                pltpu.SemaphoreType.DMA((4,)),
                pltpu.VMEM((tall, 16, side), bf16),
                pltpu.VMEM((tall, 16, side), bf16),
                pltpu.VMEM((bands, 256, side), f32),
                pltpu.VMEM((side, side), f32),
                pltpu.VMEM((256, 256), f32),
            ]
            + buffers * 2,
        ),
        compiler_params=pltpu.CompilerParams(vmem_limit_bytes=BIG),
        name="adjoint",
    )(entries, bands_of, plane, y, hist, table)


def gram_kernel(even, dual, image, first, second):
    channels, side = second.shape
    rows = image.shape[0] // channels
    left, right = jnp.where(even[0] == 1, rows - 1, 0), jnp.where(even[0] == 1, 0, rows - 1)
    for c in range(channels):
        first[c : c + 1, :side] = image[pl.ds(c * rows + left, 1), :]
        second[c : c + 1] = image[pl.ds(c * rows + right, 1), :]
    first[:, side:] = jnp.zeros((channels, first.shape[1] - side), f32)
    pick, match = row_maps(dual.shape[0], channels)
    high, low = split(dual[...] + sigma_step * image[...])
    full = jnp.where(match, nt(high, high) + nt(high, low) + nt(low, high), 0.0)

    def three(x):
        a, rest = split(x)
        b, c = split(x - a.astype(f32))
        return a, b, c

    half = sum(
        lax.dot_general(pick, part, (((0,), (0,)), ((), ())), preferred_element_type=f32)
        for part in three(full)
    )
    first[:, side : side + channels] = sum(jnp.dot(part, pick, preferred_element_type=f32) for part in three(half))


def packing(rows, side):
    short = 8 if rows % 8 == 0 else rows
    return short, rows // short * side, 2 * side // short


def dual_kernel(ridge, bound, even, *refs):
    *grams, image, flat_image, first, second, dual, low = refs[:-11]
    wavelet_out, lowrank_out, packed_out = refs[-11:-8]
    wavelet, lowrank, packed, beside, b_hi, b_lo, result, out_sem = refs[-8:]
    channels, rows, side = image.shape
    short, wide, spare = packing(rows, side)
    total = channels * rows
    step_rows = total // PARTS
    step_channels = channels // PARTS
    one_way, other_way = first[:, :side], second[...]
    beside[0] = jnp.where(even[0] == 1, other_way, one_way)
    beside[1] = jnp.where(even[0] == 1, one_way, other_way)

    def copy(which, part):
        source, to = ((packed, packed_out), (wavelet, wavelet_out), (lowrank, lowrank_out))[which]
        at = pl.ds(part * step_channels, step_channels)
        return pltpu.make_async_copy(source.at[at], to.at[at], out_sem.at[which, part])

    def details(part):
        for c in range(part * step_channels, (part + 1) * step_channels):
            w = dual[c]
            b = bound[c]
            step = columns(rows_between(image[c], beside[0, c : c + 1], beside[1, c : c + 1]))
            new = jnp.clip(w + sigma_step * step, -b, b)
            wavelet[c] = new
            slope = columns(tau_step * (2.0 * new - w))
            own = rows_between(slope, 0.0, 0.0)
            for h in range(rows // short):
                packed[c, :, h * side : (h + 1) * side] = own[h * short : (h + 1) * short]
            for k in range(short // 2):
                lanes = slice(k * spare, (k + 1) * spare)
                packed[c, k : k + 1, wide:] = -0.5 * slope[:1, lanes]
                packed[c, short // 2 + k : short // 2 + k + 1, wide:] = -0.5 * slope[rows - 1 :, lanes]

    gram = grams[0][...]
    for other in grams[1:]:
        gram = gram + other[...]
    ci = lax.broadcasted_iota(jnp.int32, (channels, channels), 0)
    cj = lax.broadcasted_iota(jnp.int32, (channels, channels), 1)
    identity = (ci == cj).astype(f32)
    shifted = gram + ridge * identity
    trace = jnp.sum(shifted * identity, keepdims=True)
    current = shifted / trace
    factor = 1.5 * identity - 0.5 * current
    inverse = factor
    for turn in range(1, NS_STEPS):
        current = jnp.dot(current, factor, precision=highest)
        if turn <= PARTS:
            details(turn - 1)
        factor = 1.5 * identity - 0.5 * jnp.dot(inverse, current, precision=highest)
        inverse = jnp.dot(factor, inverse, precision=highest)
    for part in range(NS_STEPS - 1, PARTS):
        details(part)
    for part in range(PARTS):
        copy(1, part).start()
    root_hi, root_lo = split(inverse * (math.sqrt(ridge) * lax.rsqrt(trace)))
    b_hi[...], b_lo[...] = split(low[...] + sigma_step * flat_image[...])
    pick, match = row_maps(total, channels)
    half = total // HALVES

    for h in range(HALVES):
        at = slice(h * half, (h + 1) * half)

        def spread(x):
            narrow = jnp.dot(pick[at], x, preferred_element_type=f32).astype(bf16)
            return jnp.where(match[at], nt(narrow, pick), 0.0).astype(bf16)

        result[...] = dot3(spread(root_hi), spread(root_lo), b_hi[...], b_lo[...])
        for part in range(h * PARTS // HALVES, (h + 1) * PARTS // HALVES):
            for c in range(part * step_channels, (part + 1) * step_channels):
                mine = result[c * rows - h * half : (c + 1) * rows - h * half]
                lowrank[c] = mine
                more = tau_step * (2.0 * mine - low[c * rows : (c + 1) * rows])
                for i in range(rows // short):
                    packed[c, :, i * side : (i + 1) * side] += more[i * short : (i + 1) * short]
            copy(0, part).start()
            copy(2, part).start()
    for which in range(3):
        for part in range(PARTS):
            copy(which, part).wait()


def shift_lanes(x):
    wide = x.shape[-1]
    lane = lax.broadcasted_iota(jnp.int32, x.shape, 1)
    before = jnp.where(lane == 0, 0.0, pltpu.roll(x, 1, 1))
    after = jnp.where(lane == wide - 1, 0.0, pltpu.roll(x, wide - 1, 1))
    return before + after


def columns(x):
    return x - 0.5 * shift_lanes(x)


def rows_between(x, above, below):
    height = x.shape[0]
    row = lax.broadcasted_iota(jnp.int32, x.shape, 0)
    up = jnp.where(row == 0, above, pltpu.roll(x, 1, 0))
    down = jnp.where(row == height - 1, below, pltpu.roll(x, height - 1, 0))
    return x - 0.5 * (up + down)


def row_maps(total, channels, start=0, count=None):
    rows = total // channels
    count = total if count is None else count
    si = lax.broadcasted_iota(jnp.int32, (count, channels), 0) + start
    sj = lax.broadcasted_iota(jnp.int32, (count, channels), 1)
    pick = ((si >= sj * rows) & (si < sj * rows + rows)).astype(f32).astype(bf16)
    i = lax.rem(lax.broadcasted_iota(jnp.int32, (count, 1), 0), rows)
    j = lax.rem(lax.broadcasted_iota(jnp.int32, (1, total), 1), rows)
    return pick, i == j


def local_gram(even, dual, image, channels):
    side = image.shape[1]
    lanes = side + -(-channels // 128) * 128
    return pl.pallas_call(
        gram_kernel,
        out_shape=[jax.ShapeDtypeStruct((channels, n), f32) for n in (lanes, side)],
        in_specs=[pl.BlockSpec(memory_space=pltpu.SMEM)] + whole(2),
        out_specs=whole(2),
        compiler_params=pltpu.CompilerParams(vmem_limit_bytes=12 * MIB),
        name="gram",
    )(even, dual, image)


def final_kernel(base_in, sent_in, out_ref, base, sent, out, base_sem, sent_sem, out_sem):
    devices, short, lanes = sent.shape
    side = base.shape[1]
    rows = base.shape[0] // devices
    _, wide, spare = packing(rows, side)
    step = devices // PARTS

    def reads(part):
        at, to = pl.ds(part * step * rows, step * rows), pl.ds(part * step, step)
        return (
            pltpu.make_async_copy(base_in.at[at], base.at[at], base_sem.at[part]),
            pltpu.make_async_copy(sent_in.at[to], sent.at[to], sent_sem.at[part]),
        )

    def write(part):
        at = pl.ds(part * step * rows, step * rows)
        return pltpu.make_async_copy(out.at[at], out_ref.at[at], out_sem.at[part])

    def beside(d, first):
        return jnp.concatenate([sent[d, first + k : first + k + 1, wide:] for k in range(short // 2)], axis=1)

    def wait(part):
        for read in reads(part):
            read.wait()

    for part in range(PARTS):
        for read in reads(part):
            read.start()
    wait(0)
    row = lax.broadcasted_iota(jnp.int32, (short, side), 0)
    for part in range(PARTS):
        if part + 1 < PARTS:
            wait(part + 1)
        for d in range(part * step, (part + 1) * step):
            for h in range(rows // short):
                at = slice(d * rows + h * short, d * rows + (h + 1) * short)
                left = base[at] - sent[d, :, h * side : (h + 1) * side]
                if h == 0 and d > 0:
                    left = jnp.where(row == 0, left - beside(d - 1, short // 2), left)
                if (h + 1) * short == rows and d + 1 < devices:
                    left = jnp.where(row == short - 1, left - beside(d + 1, 0), left)
                out[at] = jnp.maximum(left, 0.0)
        write(part).start()
    for part in range(PARTS):
        write(part).wait()


def final_image(base, sent):
    return pl.pallas_call(
        final_kernel,
        out_shape=jax.ShapeDtypeStruct(base.shape, f32),
        in_specs=in_hbm(2),
        out_specs=in_hbm(1)[0],
        scratch_shapes=[
            pltpu.VMEM(base.shape, f32),
            pltpu.VMEM(sent.shape, f32),
            pltpu.VMEM(base.shape, f32),
        ]
        + [pltpu.SemaphoreType.DMA((PARTS,))] * 3,
        input_output_aliases={0: 0},
        compiler_params=pltpu.CompilerParams(vmem_limit_bytes=8 * MIB),
        name="final",
    )(base, sent)


def dual_update(ridge, bound, even, grams, image, first, second, dual, low):
    channels, rows, side = image.shape
    flat = (channels * rows, side)
    short, wide, spare = packing(rows, side)
    packed = (channels, short, wide + spare)
    smem = pl.BlockSpec(memory_space=pltpu.SMEM)
    return pl.pallas_call(
        functools.partial(dual_kernel, ridge),
        out_shape=[jax.ShapeDtypeStruct(image.shape, f32)] * 2 + [jax.ShapeDtypeStruct(packed, f32)],
        in_specs=[smem, smem] + whole(len(grams) + 6),
        out_specs=in_hbm(3),
        scratch_shapes=[
            pltpu.VMEM(image.shape, f32),
            pltpu.VMEM(image.shape, f32),
            pltpu.VMEM(packed, f32),
            pltpu.VMEM((2, channels, side), f32),
            pltpu.VMEM(flat, bf16),
            pltpu.VMEM(flat, bf16),
            pltpu.VMEM((flat[0] // HALVES, side), f32),
            pltpu.SemaphoreType.DMA((3, PARTS)),
        ],
        compiler_params=pltpu.CompilerParams(vmem_limit_bytes=24 * MIB),
        name="dual",
    )(bound, even, *grams, image, image.reshape(flat), first, second, dual, low.reshape(flat))


def per_device(
    image, visibilities, tile_index, cells, block_count, lowrank_dual, wavelet_dual, wavelet_bound
):
    side = image.shape[-1]
    channels, rows_here, _ = lowrank_dual.shape
    devices = lax.axis_size(RING)
    pieces = lax.axis_size("pix")
    flat = (channels * rows_here, side)

    facet_image = lax.all_to_all(
        image.reshape(devices, rows_here, side), RING, split_axis=0, concat_axis=0, tiled=True
    )

    bands = 2 * side // TILE_C
    chunks = tile_index.shape[1] // GROUP + bands + 1
    table, sizes = small_tables(side, side)
    table = jnp.asarray(table)
    entries, bands_of = plan_blocks(tile_index[0], block_count[0], bands, chunks)
    y, hist = forward(image[0], visibilities[:, 0], cells[0], block_count, table, sizes)
    even = (1 - lax.axis_index(RING) % 2).astype(jnp.int32)[None]
    facet_image, y, entries, bands_of, even = lax.optimization_barrier(
        (facet_image, y, entries, bands_of, even)
    )

    first, second = local_gram(even, lowrank_dual.reshape(flat), facet_image.reshape(flat), channels)
    first_got = lax.ppermute(first, RING, [(i, i ^ 1) for i in range(devices)])
    inner = [(i, i + 1) for i in range(1, devices - 1, 2)]
    second_got = lax.ppermute(second, RING, inner + [(j, i) for i, j in inner])
    grams = [first[:, side : side + channels], first_got[:, side : side + channels]]
    for turn in range(1, pieces.bit_length() - 1):
        gram = sum(grams)
        grams = [gram, lax.ppermute(gram, "pix", [(i, i ^ (1 << turn)) for i in range(pieces)])]
    ridge = float(rows_here * side * pieces)
    wavelet_next, lowrank_next, packed = dual_update(
        ridge, wavelet_bound, even, grams, facet_image, first_got, second_got, wavelet_dual, lowrank_dual
    )
    packed, y = lax.optimization_barrier((packed, y))
    returned = lax.all_to_all(packed, RING, split_axis=0, concat_axis=0, tiled=True)
    base = adjoint(entries, bands_of, image[0], y, hist, table, sizes)
    image_next = final_image(base, returned)
    return (image_next[None], lowrank_next, wavelet_next)


def solution(mesh):
    return jax.shard_map(
        per_device,
        mesh=mesh,
        in_specs=(
            P(RING, None, None),
            P(None, RING, None, None),
            P(RING, None),
            P(RING, None, None),
            P(RING),
            P(None, RING, None),
            P(None, RING, None),
            P(),
        ),
        out_specs=(P(RING, None, None), P(None, RING, None), P(None, RING, None)),
        check_vma=False,
    )
```

```python
import functools
import math

import jax
import jax.numpy as jnp
import numpy as np
from jax import lax
from jax.experimental import pallas as pl
from jax.experimental.pallas import tpu as pltpu
from jax.sharding import PartitionSpec as P

TILE_R = 8
TILE_C = 128
NS_STEPS = 5
GROUP = 16
PARTS = 4
HALVES = 1
PIECES = 4
RING = ("facet", "pix")

highest = lax.Precision.HIGHEST
tau_step = 0.5
sigma_step = 1.0
f32 = jnp.float32
bf16 = jnp.bfloat16
MIB = 1024 * 1024
BIG = 58 * MIB


def gauss(n):
    d = np.arange(n)[:, None] - np.arange(n)[None, :]
    return np.exp(-0.5 * d.astype(np.float64) ** 2)


def small_tables(height, width):
    rows, cols = 2 * height, 2 * width
    m = np.arange(height)
    n = np.arange(width)
    near = gauss(TILE_R) @ np.exp(-2j * np.pi * np.arange(TILE_R)[:, None] * m[None, :] / rows)
    period = rows // TILE_R
    turn = np.exp(
        -2j * np.pi * (np.arange(period)[:, None] * np.arange(period)[None, :] % period) / period
    )
    span = np.exp(-2j * np.pi * n[:, None] * np.arange(TILE_C)[None, :] / cols) @ gauss(TILE_C)
    span = span / height
    bands = cols // TILE_C
    swing = np.exp(-2j * np.pi * np.arange(bands)[:, None] * np.arange(8)[None, :] / bands)
    swing = np.broadcast_to(swing[:, :, None], (bands, 8, TILE_C))
    assert bands == 8 and period == 128
    near = near.reshape(TILE_R, -1, 128).transpose(1, 0, 2)
    parts = []
    for table in (span, swing, turn, near):
        parts += [table.real.reshape(-1, 128), table.imag.reshape(-1, 128)]
    return np.concatenate(parts).astype(np.float32), [len(part) for part in parts]


def table_views(table, sizes):
    views, start = [], 0
    for size in sizes:
        views.append(table.at[pl.ds(start, size)])
        start += size
    return views


def split(x):
    high = x.astype(bf16)
    return high, (x - high.astype(f32)).astype(bf16)


def dot3(a_hi, a_lo, b_hi, b_lo):
    return (
        jnp.dot(a_hi, b_hi, preferred_element_type=f32)
        + jnp.dot(a_lo, b_hi, preferred_element_type=f32)
        + jnp.dot(a_hi, b_lo, preferred_element_type=f32)
    )


def nt(a, b):
    return lax.dot_general(a, b, (((1,), (1,)), ((), ())), preferred_element_type=f32)


def plan_blocks(tiles, count, bands, chunks):
    blocks = tiles.shape[0]
    index = jnp.arange(blocks, dtype=jnp.int32)
    band = jnp.where(index < count, tiles % bands, bands)
    same = band[:, None] == band[None, :]
    rank = jnp.sum((same & (index[None, :] < index[:, None])).astype(jnp.int32), axis=1)
    sizes = jnp.sum((band[None, :] == jnp.arange(bands, dtype=jnp.int32)[:, None]).astype(jnp.int32), axis=1)
    groups = (sizes + GROUP - 1) // GROUP
    upto = jnp.arange(bands)[None, :] <= jnp.arange(bands)[:, None]
    ends = jnp.sum(jnp.where(upto, groups[None, :], 0), axis=1)
    first = ends - groups
    mine = band[:, None] == jnp.arange(bands, dtype=jnp.int32)[None, :]
    slot = jnp.sum(jnp.where(mine, first[None, :] * GROUP, 0), axis=1) + rank
    slot = jnp.where(band < bands, slot, -1)
    spots = jnp.arange(chunks * GROUP, dtype=jnp.int32)
    code = index * 128 + tiles // bands
    spare = blocks * 128
    entries = spare + jnp.sum(jnp.where(slot[None, :] == spots[:, None], code[None, :] - spare, 0), axis=1)
    which = jnp.sum((jnp.arange(chunks)[:, None] >= ends[None, :]).astype(jnp.int32), axis=1)
    which = jnp.minimum(which, bands - 1)
    return entries.astype(jnp.int32), jnp.concatenate([which, ends[-1:]]).astype(jnp.int32)


def column_band(b, span_re, span_im, swing_re, swing_im):
    side = span_re.shape[0]
    at = pl.ds(pl.multiple_of(b * 8, 8), 8)
    cr = swing_re[at][None]
    ci = swing_im[at][None]
    sr = span_re[...].reshape(side // 8, 8, TILE_C)
    si = span_im[...].reshape(side // 8, 8, TILE_C)
    re = (cr * sr - ci * si).reshape(side, TILE_C)
    im = (cr * si + ci * sr).reshape(side, TILE_C)
    return split(jnp.concatenate([re, im], axis=1))


def forward_kernel(
    sizes, live, image_in, cells_in, vis_in, table_in, y_out, hist_out,
    image, cells, vis, table, y, hist, x_hi, x_lo, in_sem, y_sem, hist_sem, spare_sem,
):
    bands = y.shape[1]
    blocks = cells.shape[0]
    reads = [
        pltpu.make_async_copy(source, to, in_sem.at[i])
        for i, (source, to) in enumerate(
            ((image_in, image), (table_in.at[pl.ds(0, table.shape[0])], table), (cells_in, cells), (vis_in, vis))
        )
    ]
    for read in reads:
        read.start()
    span_re, span_im, swing_re, swing_im = table_views(table, sizes)
    reads[0].wait()
    x_hi[...], x_lo[...] = split(image[...])
    reads[1].wait()

    def y_copy(part, b):
        return pltpu.make_async_copy(y.at[part, b], y_out.at[part, b], y_sem.at[part, b])

    def hist_copy(g):
        at = pl.ds(g * GROUP, GROUP)
        return pltpu.make_async_copy(hist.at[at], hist_out.at[at], hist_sem.at[g])

    def build_cols(b, carry):
        high, low = column_band(b, span_re, span_im, swing_re, swing_im)
        high, low = split(dot3(x_hi[...], x_lo[...], high, low))
        y[0, b] = high
        y[1, b] = low
        y_copy(0, b).start()
        y_copy(1, b).start()
        return carry

    lax.fori_loop(0, bands, build_cols, 0, unroll=2)

    reads[2].wait()
    reads[3].wait()
    hist[blocks] = jnp.zeros((24, 128), f32)
    spare = pltpu.make_async_copy(hist.at[pl.ds(blocks, 1)], hist_out.at[pl.ds(blocks, 1)], spare_sem)
    spare.start()
    rows8 = lax.broadcasted_iota(jnp.int32, (8, 128), 0)
    rows128 = lax.broadcasted_iota(jnp.int32, (128, 128), 0)

    def count_cells(g, carry):
        base = pl.multiple_of(g * GROUP, GROUP)
        q = cells[pl.ds(base, GROUP), :]
        qr = q // TILE_C
        qc = q - qr * TILE_C
        parts = []
        for p in range(2):
            v = vis[p, pl.ds(base, GROUP), :]
            high = v.astype(bf16).astype(f32)
            parts += [high, v - high]
        for s in range(GROUP):
            row = (rows8 == qr[s : s + 1]).astype(f32)
            pieces = [row] + [row * part[s : s + 1] for part in parts]
            lhs = jnp.concatenate(pieces + [jnp.zeros((8, 128), f32)], axis=0).astype(bf16)
            hot = (rows128 == qc[s : s + 1]).astype(f32).astype(bf16)
            out = nt(lhs, hot)
            hist[base + s, 0:8] = out[0:8]
            hist[base + s, 8:16] = out[8:16] + out[16:24]
            hist[base + s, 16:24] = out[24:32] + out[32:40]
        hist_copy(g).start()
        return carry

    groups = (live[0] + GROUP - 1) // GROUP
    lax.fori_loop(0, groups, count_cells, 0)

    def hist_wait(g, carry):
        hist_copy(g).wait()
        return carry

    lax.fori_loop(0, groups, hist_wait, 0)
    spare.wait()
    for part in range(2):
        for b in range(bands):
            y_copy(part, b).wait()


def adjoint_kernel(
    sizes, entries, bands_of, image_in, y_in, hist_in, table_in,
    out, image, y, hist, table, sems, wt_hi, wt_lo, z, acc, r_ref, *sets,
):
    side = image.shape[0]
    bands = y.shape[1]
    chunks = entries.shape[0] // GROUP
    reads = [
        pltpu.make_async_copy(source, to, sems.at[i])
        for i, (source, to) in enumerate(((table_in, table), (y_in, y), (hist_in, hist), (image_in, image)))
    ]
    for read in reads:
        read.start()
    span_re, span_im, swing_re, swing_im, turn_re, turn_im, near_re, near_im = table_views(table, sizes)
    reads[0].wait()
    tall = wt_hi.shape[0]
    sets = (sets[:3], sets[3:])

    def build_rows(a, carry):
        pr = jnp.broadcast_to(turn_re[pl.ds(a, 1), :], (8, 128))
        pi = jnp.broadcast_to(turn_im[pl.ds(a, 1), :], (8, 128))
        for t in range(side // 128):
            at = slice(t * 128, (t + 1) * 128)
            nr, ni = near_re[8 * t : 8 * t + 8], near_im[8 * t : 8 * t + 8]
            both = jnp.concatenate([pr * nr - pi * ni, pr * ni + pi * nr], axis=0)
            high, low = split(both)
            wt_hi[a, :, at] = high
            wt_lo[a, :, at] = low
        return carry

    lax.fori_loop(0, tall, build_rows, 0, unroll=4)
    z[...] = jnp.zeros_like(z)
    for read in reads[1:]:
        read.wait()

    def evaluate(c, refs):
        wg_hi, wg_lo, o_ref = refs
        b = bands_of[c]
        for s in range(GROUP):
            a = entries[c * GROUP + s] & 127
            wg_hi[16 * s : 16 * s + 16] = wt_hi[a]
            wg_lo[16 * s : 16 * s + 16] = wt_lo[a]
        o_ref[...] = dot3(wg_hi[...], wg_lo[...], y[0, b], y[1, b])

    def spread(c, refs):
        wg_hi, wg_lo, o_ref = refs
        for s in range(GROUP):
            k = entries[c * GROUP + s] // 128
            top = slice(16 * s, 16 * s + 8)
            low = slice(16 * s + 8, 16 * s + 16)
            model_re = o_ref[top, 0:128] - o_ref[low, 128:256]
            model_im = o_ref[top, 128:256] + o_ref[low, 0:128]
            many = hist[k, 0:8]
            g_re = many * model_re - hist[k, 8:16]
            g_im = many * model_im - hist[k, 16:24]
            r_ref[top, 0:128] = g_re
            r_ref[top, 128:256] = g_im
            r_ref[low, 0:128] = g_im
            r_ref[low, 128:256] = -g_re
        rt_hi, rt_lo = split(r_ref[...].T)
        z[bands_of[c]] += dot3(rt_hi, rt_lo, wg_hi[...], wg_lo[...])

    evaluate(0, sets[0])

    def work(i, carry):
        evaluate(2 * i + 1, sets[1])
        spread(2 * i, sets[0])
        evaluate(2 * i + 2, sets[0])
        spread(2 * i + 1, sets[1])
        return carry

    lax.fori_loop(0, (bands_of[chunks] + 1) // 2, work, 0)
    acc[...] = jnp.zeros_like(acc)

    def back(b, carry):
        wc_hi, wc_lo = column_band(b, span_re, span_im, swing_re, swing_im)
        high, low = split(z[b])
        acc[...] += dot3(wc_hi, wc_lo, high, low)
        return carry

    lax.fori_loop(0, bands, back, 0, unroll=2)
    out[...] = image[...] - tau_step * acc[...].T


def whole(n):
    return [pl.BlockSpec(memory_space=pltpu.VMEM) for _ in range(n)]


def in_hbm(n):
    return [pl.BlockSpec(memory_space=pltpu.HBM) for _ in range(n)]


def forward(plane, vis, cells, count, table, sizes):
    side = plane.shape[0]
    bands = 2 * side // TILE_C
    blocks = cells.shape[0]
    y = (2, bands, side, 256)
    hist = (blocks + 1, 24, 128)
    return pl.pallas_call(
        functools.partial(forward_kernel, sizes[:4]),
        out_shape=[jax.ShapeDtypeStruct(y, bf16), jax.ShapeDtypeStruct(hist, f32)],
        grid_spec=pltpu.PrefetchScalarGridSpec(
            num_scalar_prefetch=1,
            grid=(),
            in_specs=in_hbm(4),
            out_specs=in_hbm(2),
            scratch_shapes=[
                pltpu.VMEM(plane.shape, f32),
                pltpu.VMEM(cells.shape, jnp.int32),
                pltpu.VMEM(vis.shape, f32),
                pltpu.VMEM((sum(sizes[:4]), 128), f32),
                pltpu.VMEM(y, bf16),
                pltpu.VMEM(hist, f32),
                pltpu.VMEM((side, side), bf16),
                pltpu.VMEM((side, side), bf16),
                pltpu.SemaphoreType.DMA((4,)),
                pltpu.SemaphoreType.DMA((2, bands)),
                pltpu.SemaphoreType.DMA((blocks // GROUP,)),
                pltpu.SemaphoreType.DMA,
            ],
        ),
        compiler_params=pltpu.CompilerParams(vmem_limit_bytes=BIG),
        name="forward",
    )(count, plane, cells, vis, table)


def adjoint(entries, bands_of, plane, y, hist, table, sizes):
    _, bands, side, _ = y.shape
    tall = 2 * side // TILE_R
    buffers = [pltpu.VMEM((256, side), bf16), pltpu.VMEM((256, side), bf16), pltpu.VMEM((256, 256), f32)]
    return pl.pallas_call(
        functools.partial(adjoint_kernel, sizes),
        out_shape=jax.ShapeDtypeStruct((side, side), f32),
        grid_spec=pltpu.PrefetchScalarGridSpec(
            num_scalar_prefetch=2,
            grid=(),
            in_specs=in_hbm(4),
            out_specs=whole(1)[0],
            scratch_shapes=[
                pltpu.VMEM(plane.shape, f32),
                pltpu.VMEM(y.shape, bf16),
                pltpu.VMEM(hist.shape, f32),
                pltpu.VMEM(table.shape, f32),
                pltpu.SemaphoreType.DMA((4,)),
                pltpu.VMEM((tall, 16, side), bf16),
                pltpu.VMEM((tall, 16, side), bf16),
                pltpu.VMEM((bands, 256, side), f32),
                pltpu.VMEM((side, side), f32),
                pltpu.VMEM((256, 256), f32),
            ]
            + buffers * 2,
        ),
        compiler_params=pltpu.CompilerParams(vmem_limit_bytes=BIG),
        name="adjoint",
    )(entries, bands_of, plane, y, hist, table)


def edge_kernel(even, image, second):
    channels = second.shape[0]
    rows = image.shape[0] // channels
    at = jnp.where(even[0] == 1, 0, rows - 1)
    for c in range(channels):
        second[c : c + 1] = image[pl.ds(c * rows + at, 1), :]


def gram_kernel(even, dual, image, first):
    channels = first.shape[0]
    side = image.shape[1]
    rows = image.shape[0] // channels
    at = jnp.where(even[0] == 1, rows - 1, 0)
    for c in range(channels):
        first[c : c + 1, :side] = image[pl.ds(c * rows + at, 1), :]
    first[:, side:] = jnp.zeros((channels, first.shape[1] - side), f32)
    pick, match = row_maps(dual.shape[0], channels)
    high, low = split(dual[...] + sigma_step * image[...])
    full = jnp.where(match, nt(high, high) + nt(high, 2.0 * low), 0.0)
    half = sum(
        lax.dot_general(pick, part, (((0,), (0,)), ((), ())), preferred_element_type=f32)
        for part in split(full)
    )
    gram = sum(jnp.dot(part, pick, preferred_element_type=f32) for part in split(half))
    first[:, side : side + channels] = 0.5 * (gram + gram.T)


def packing(rows, side):
    short = 8 if rows % 8 == 0 else rows
    return short, rows // short * side, 2 * side // short


def dual_kernel(ridge, bound, even, *refs):
    *grams, image, flat_image, first, second, dual, low = refs[:-11]
    wavelet_out, lowrank_out, packed_out = refs[-11:-8]
    wavelet, lowrank, packed, beside, b_hi, b_lo, result, out_sem = refs[-8:]
    channels, rows, side = image.shape
    short, wide, spare = packing(rows, side)
    total = channels * rows
    step_rows = total // PARTS
    step_channels = channels // PARTS
    one_way, other_way = first[:, :side], second[...]
    beside[0] = jnp.where(even[0] == 1, other_way, one_way)
    beside[1] = jnp.where(even[0] == 1, one_way, other_way)

    def copy(which, part):
        source, to = ((packed, packed_out), (wavelet, wavelet_out), (lowrank, lowrank_out))[which]
        at = pl.ds(part * step_channels, step_channels)
        return pltpu.make_async_copy(source.at[at], to.at[at], out_sem.at[which, part])

    def details(part):
        for c in range(part * step_channels, (part + 1) * step_channels):
            w = dual[c]
            b = bound[c]
            step = columns(rows_between(image[c], beside[0, c : c + 1], beside[1, c : c + 1]))
            new = jnp.clip(w + sigma_step * step, -b, b)
            wavelet[c] = new
            slope = columns(tau_step * (2.0 * new - w))
            own = rows_between(slope, 0.0, 0.0)
            for h in range(rows // short):
                packed[c, :, h * side : (h + 1) * side] = own[h * short : (h + 1) * short]
            for k in range(short // 2):
                lanes = slice(k * spare, (k + 1) * spare)
                packed[c, k : k + 1, wide:] = -0.5 * slope[:1, lanes]
                packed[c, short // 2 + k : short // 2 + k + 1, wide:] = -0.5 * slope[rows - 1 :, lanes]

    pick, match = row_maps(total, channels)
    b_hi[...], b_lo[...] = split(low[...] + sigma_step * flat_image[...])
    gram = grams[0][...]
    for other in grams[1:]:
        gram = gram + other[...]
    ci = lax.broadcasted_iota(jnp.int32, (channels, channels), 0)
    cj = lax.broadcasted_iota(jnp.int32, (channels, channels), 1)
    identity = (ci == cj).astype(f32)
    shifted = gram + ridge * identity
    trace = jnp.sum(shifted * identity, keepdims=True)
    current = shifted / trace
    factor = 1.5 * identity - 0.5 * current
    inverse = factor
    for turn in range(1, NS_STEPS):
        current = jnp.dot(current, factor, precision=highest)
        if turn <= PARTS:
            details(turn - 1)
        factor = 1.5 * identity - 0.5 * jnp.dot(inverse, current, precision=highest)
        inverse = jnp.dot(factor, inverse, precision=highest)
    for part in range(NS_STEPS - 1, PARTS):
        details(part)
    for part in range(PARTS):
        copy(1, part).start()
    root_hi, root_lo = split(inverse * (math.sqrt(ridge) * lax.rsqrt(trace)))
    half = total // HALVES

    for h in range(HALVES):
        at = slice(h * half, (h + 1) * half)

        def spread(x):
            narrow = jnp.dot(pick[at], x, preferred_element_type=f32).astype(bf16)
            return jnp.where(match[at], nt(narrow, pick), 0.0).astype(bf16)

        result[...] = dot3(spread(root_hi), spread(root_lo), b_hi[...], b_lo[...])
        for part in range(h * PARTS // HALVES, (h + 1) * PARTS // HALVES):
            for c in range(part * step_channels, (part + 1) * step_channels):
                mine = result[c * rows - h * half : (c + 1) * rows - h * half]
                lowrank[c] = mine
                more = tau_step * (2.0 * mine - low[c * rows : (c + 1) * rows])
                for i in range(rows // short):
                    packed[c, :, i * side : (i + 1) * side] += more[i * short : (i + 1) * short]
            copy(0, part).start()
            copy(2, part).start()
    for which in range(3):
        for part in range(PARTS):
            copy(which, part).wait()


def shift_lanes(x):
    wide = x.shape[-1]
    lane = lax.broadcasted_iota(jnp.int32, x.shape, 1)
    before = jnp.where(lane == 0, 0.0, pltpu.roll(x, 1, 1))
    after = jnp.where(lane == wide - 1, 0.0, pltpu.roll(x, wide - 1, 1))
    return before + after


def columns(x):
    return x - 0.5 * shift_lanes(x)


def rows_between(x, above, below):
    height = x.shape[0]
    row = lax.broadcasted_iota(jnp.int32, x.shape, 0)
    up = jnp.where(row == 0, above, pltpu.roll(x, 1, 0))
    down = jnp.where(row == height - 1, below, pltpu.roll(x, height - 1, 0))
    return x - 0.5 * (up + down)


def row_maps(total, channels, start=0, count=None):
    rows = total // channels
    count = total if count is None else count
    si = lax.broadcasted_iota(jnp.int32, (count, channels), 0) + start
    sj = lax.broadcasted_iota(jnp.int32, (count, channels), 1)
    pick = ((si >= sj * rows) & (si < sj * rows + rows)).astype(f32).astype(bf16)
    i = lax.rem(lax.broadcasted_iota(jnp.int32, (count, 1), 0), rows)
    j = lax.rem(lax.broadcasted_iota(jnp.int32, (1, total), 1), rows)
    return pick, i == j


def edge_rows(even, image, channels):
    return pl.pallas_call(
        edge_kernel,
        out_shape=jax.ShapeDtypeStruct((channels, image.shape[1]), f32),
        in_specs=[pl.BlockSpec(memory_space=pltpu.SMEM)] + whole(1),
        out_specs=whole(1)[0],
        compiler_params=pltpu.CompilerParams(vmem_limit_bytes=8 * MIB),
        name="edge",
    )(even, image)


def local_gram(even, dual, image, channels):
    lanes = image.shape[1] + -(-channels // 128) * 128
    return pl.pallas_call(
        gram_kernel,
        out_shape=jax.ShapeDtypeStruct((channels, lanes), f32),
        in_specs=[pl.BlockSpec(memory_space=pltpu.SMEM)] + whole(2),
        out_specs=whole(1)[0],
        compiler_params=pltpu.CompilerParams(vmem_limit_bytes=12 * MIB),
        name="gram",
    )(even, dual, image)


def final_kernel(base_in, sent, out_ref, base, base_sem, out_sem):
    devices, short, _ = sent.shape
    side = base.shape[1]
    rows = base.shape[0] // devices
    _, wide, spare = packing(rows, side)
    step = devices // PIECES

    def read(part):
        at = pl.ds(part * step * rows, step * rows)
        return pltpu.make_async_copy(base_in.at[at], base.at[at], base_sem.at[part])

    def write(part):
        at = pl.ds(part * step * rows, step * rows)
        return pltpu.make_async_copy(base.at[at], out_ref.at[at], out_sem.at[part])

    def beside(d, first):
        return jnp.concatenate([sent[d, first + k : first + k + 1, wide:] for k in range(short // 2)], axis=1)

    for part in range(PIECES):
        read(part).start()
    row = lax.broadcasted_iota(jnp.int32, (short, side), 0)
    for part in range(PIECES):
        read(part).wait()
        for d in range(part * step, (part + 1) * step):
            for h in range(rows // short):
                at = slice(d * rows + h * short, d * rows + (h + 1) * short)
                left = base[at] - sent[d, :, h * side : (h + 1) * side]
                if h == 0 and d > 0:
                    left = jnp.where(row == 0, left - beside(d - 1, short // 2), left)
                if (h + 1) * short == rows and d + 1 < devices:
                    left = jnp.where(row == short - 1, left - beside(d + 1, 0), left)
                base[at] = jnp.maximum(left, 0.0)
        write(part).start()
    for part in range(PIECES):
        write(part).wait()


def final_image(base, sent):
    return pl.pallas_call(
        final_kernel,
        out_shape=jax.ShapeDtypeStruct(base.shape, f32),
        in_specs=in_hbm(1) + whole(1),
        out_specs=in_hbm(1)[0],
        scratch_shapes=[pltpu.VMEM(base.shape, f32)] + [pltpu.SemaphoreType.DMA((PIECES,))] * 2,
        input_output_aliases={0: 0},
        compiler_params=pltpu.CompilerParams(vmem_limit_bytes=8 * MIB),
        name="final",
    )(base, sent)


def dual_update(ridge, bound, even, grams, image, first, second, dual, low):
    channels, rows, side = image.shape
    flat = (channels * rows, side)
    short, wide, spare = packing(rows, side)
    packed = (channels, short, wide + spare)
    smem = pl.BlockSpec(memory_space=pltpu.SMEM)
    return pl.pallas_call(
        functools.partial(dual_kernel, ridge),
        out_shape=[jax.ShapeDtypeStruct(image.shape, f32)] * 2 + [jax.ShapeDtypeStruct(packed, f32)],
        in_specs=[smem, smem] + whole(len(grams) + 6),
        out_specs=in_hbm(3),
        scratch_shapes=[
            pltpu.VMEM(image.shape, f32),
            pltpu.VMEM(image.shape, f32),
            pltpu.VMEM(packed, f32),
            pltpu.VMEM((2, channels, side), f32),
            pltpu.VMEM(flat, bf16),
            pltpu.VMEM(flat, bf16),
            pltpu.VMEM((flat[0] // HALVES, side), f32),
            pltpu.SemaphoreType.DMA((3, PARTS)),
        ],
        compiler_params=pltpu.CompilerParams(vmem_limit_bytes=24 * MIB),
        name="dual",
    )(bound, even, *grams, image, image.reshape(flat), first, second, dual, low.reshape(flat))


def per_device(
    image, visibilities, tile_index, cells, block_count, lowrank_dual, wavelet_dual, wavelet_bound
):
    side = image.shape[-1]
    channels, rows_here, _ = lowrank_dual.shape
    devices = lax.axis_size(RING)
    pieces = lax.axis_size("pix")
    flat = (channels * rows_here, side)

    facet_image = lax.all_to_all(
        image.reshape(devices, rows_here, side), RING, split_axis=0, concat_axis=0, tiled=True
    )

    bands = 2 * side // TILE_C
    chunks = tile_index.shape[1] // GROUP + bands + 1
    table, sizes = small_tables(side, side)
    table = jnp.asarray(table)
    entries, bands_of = plan_blocks(tile_index[0], block_count[0], bands, chunks)
    y, hist = forward(image[0], visibilities[:, 0], cells[0], block_count, table, sizes)
    even = (1 - lax.axis_index(RING) % 2).astype(jnp.int32)[None]
    facet_image, y, entries, bands_of, even = lax.optimization_barrier(
        (facet_image, y, entries, bands_of, even)
    )

    inner = [(i, i + 1) for i in range(1, devices - 1, 2)]
    second = edge_rows(even, facet_image.reshape(flat), channels)
    second_got = lax.ppermute(second, RING, inner + [(j, i) for i, j in inner])
    first = local_gram(even, lowrank_dual.reshape(flat), facet_image.reshape(flat), channels)
    first_got = lax.ppermute(first, RING, [(i, i ^ 1) for i in range(devices)])
    grams = [first[:, side : side + channels], first_got[:, side : side + channels]]
    for turn in range(1, pieces.bit_length() - 1):
        gram = sum(grams)
        grams = [gram, lax.ppermute(gram, "pix", [(i, i ^ (1 << turn)) for i in range(pieces)])]
    ridge = float(rows_here * side * pieces)
    wavelet_next, lowrank_next, packed = dual_update(
        ridge, wavelet_bound, even, grams, facet_image, first_got, second_got, wavelet_dual, lowrank_dual
    )
    packed, y = lax.optimization_barrier((packed, y))
    returned = lax.all_to_all(packed, RING, split_axis=0, concat_axis=0, tiled=True)
    base = adjoint(entries, bands_of, image[0], y, hist, table, sizes)
    image_next = final_image(base, returned)
    return (image_next[None], lowrank_next, wavelet_next)


def solution(mesh):
    return jax.shard_map(
        per_device,
        mesh=mesh,
        in_specs=(
            P(RING, None, None),
            P(None, RING, None, None),
            P(RING, None),
            P(RING, None, None),
            P(RING),
            P(None, RING, None),
            P(None, RING, None),
            P(),
        ),
        out_specs=(P(RING, None, None), P(None, RING, None), P(None, RING, None)),
        check_vma=False,
    )
```

```python
import functools
import math

import jax
import jax.numpy as jnp
import numpy as np
from jax import lax
from jax.experimental import pallas as pl
from jax.experimental.pallas import tpu as pltpu
from jax.sharding import PartitionSpec as P

TILE_R = 8
TILE_C = 128
NS_STEPS = 5
GROUP = 16
PARTS = 4
HALVES = 1
PIECES = 4
RING = ("facet", "pix")

highest = lax.Precision.HIGHEST
tau_step = 0.5
sigma_step = 1.0
f32 = jnp.float32
bf16 = jnp.bfloat16
MIB = 1024 * 1024
BIG = 58 * MIB


def gauss(n):
    d = np.arange(n)[:, None] - np.arange(n)[None, :]
    return np.exp(-0.5 * d.astype(np.float64) ** 2)


def small_tables(height, width):
    rows, cols = 2 * height, 2 * width
    m = np.arange(height)
    n = np.arange(width)
    near = gauss(TILE_R) @ np.exp(-2j * np.pi * np.arange(TILE_R)[:, None] * m[None, :] / rows)
    period = rows // TILE_R
    turn = np.exp(
        -2j * np.pi * (np.arange(period)[:, None] * np.arange(period)[None, :] % period) / period
    )
    span = np.exp(-2j * np.pi * n[:, None] * np.arange(TILE_C)[None, :] / cols) @ gauss(TILE_C)
    span = span / height
    bands = cols // TILE_C
    swing = np.exp(-2j * np.pi * np.arange(bands)[:, None] * np.arange(8)[None, :] / bands)
    swing = np.broadcast_to(swing[:, :, None], (bands, 8, TILE_C))
    assert bands == 8 and period == 128
    near = near.reshape(TILE_R, -1, 128).transpose(1, 0, 2)
    parts = []
    for table in (span, swing, turn, near):
        parts += [table.real.reshape(-1, 128), table.imag.reshape(-1, 128)]
    return np.concatenate(parts).astype(np.float32), [len(part) for part in parts]


def table_views(table, sizes):
    views, start = [], 0
    for size in sizes:
        views.append(table.at[pl.ds(start, size)])
        start += size
    return views


def split(x):
    high = x.astype(bf16)
    return high, (x - high.astype(f32)).astype(bf16)


def dot3(a_hi, a_lo, b_hi, b_lo):
    return (
        jnp.dot(a_hi, b_hi, preferred_element_type=f32)
        + jnp.dot(a_lo, b_hi, preferred_element_type=f32)
        + jnp.dot(a_hi, b_lo, preferred_element_type=f32)
    )


def nt(a, b):
    return lax.dot_general(a, b, (((1,), (1,)), ((), ())), preferred_element_type=f32)


def plan_blocks(tiles, count, bands, chunks):
    blocks = tiles.shape[0]
    index = jnp.arange(blocks, dtype=jnp.int32)
    band = jnp.where(index < count, tiles % bands, bands)
    same = band[:, None] == band[None, :]
    rank = jnp.sum((same & (index[None, :] < index[:, None])).astype(jnp.int32), axis=1)
    sizes = jnp.sum((band[None, :] == jnp.arange(bands, dtype=jnp.int32)[:, None]).astype(jnp.int32), axis=1)
    groups = (sizes + GROUP - 1) // GROUP
    upto = jnp.arange(bands)[None, :] <= jnp.arange(bands)[:, None]
    ends = jnp.sum(jnp.where(upto, groups[None, :], 0), axis=1)
    first = ends - groups
    mine = band[:, None] == jnp.arange(bands, dtype=jnp.int32)[None, :]
    slot = jnp.sum(jnp.where(mine, first[None, :] * GROUP, 0), axis=1) + rank
    slot = jnp.where(band < bands, slot, -1)
    spots = jnp.arange(chunks * GROUP, dtype=jnp.int32)
    code = index * 128 + tiles // bands
    spare = blocks * 128
    entries = spare + jnp.sum(jnp.where(slot[None, :] == spots[:, None], code[None, :] - spare, 0), axis=1)
    which = jnp.sum((jnp.arange(chunks)[:, None] >= ends[None, :]).astype(jnp.int32), axis=1)
    which = jnp.minimum(which, bands - 1)
    return entries.astype(jnp.int32), jnp.concatenate([which, ends[-1:]]).astype(jnp.int32)


def column_band(b, span_re, span_im, swing_re, swing_im):
    side = span_re.shape[0]
    at = pl.ds(pl.multiple_of(b * 8, 8), 8)
    cr = swing_re[at][None]
    ci = swing_im[at][None]
    sr = span_re[...].reshape(side // 8, 8, TILE_C)
    si = span_im[...].reshape(side // 8, 8, TILE_C)
    re = (cr * sr - ci * si).reshape(side, TILE_C)
    im = (cr * si + ci * sr).reshape(side, TILE_C)
    return split(jnp.concatenate([re, im], axis=1))


def forward_kernel(
    sizes, live, image_in, cells_in, vis_in, table_in, y_out, hist_out,
    image, cells, vis, table, y, hist, x_hi, x_lo, in_sem, y_sem, hist_sem, spare_sem,
):
    bands = y.shape[1]
    blocks = cells.shape[0]
    reads = [
        pltpu.make_async_copy(source, to, in_sem.at[i])
        for i, (source, to) in enumerate(
            ((image_in, image), (table_in.at[pl.ds(0, table.shape[0])], table), (cells_in, cells), (vis_in, vis))
        )
    ]
    for read in reads:
        read.start()
    span_re, span_im, swing_re, swing_im = table_views(table, sizes)
    reads[0].wait()
    x_hi[...], x_lo[...] = split(image[...])
    reads[1].wait()

    def y_copy(part, b):
        return pltpu.make_async_copy(y.at[part, b], y_out.at[part, b], y_sem.at[part, b])

    def hist_copy(g):
        at = pl.ds(g * GROUP, GROUP)
        return pltpu.make_async_copy(hist.at[at], hist_out.at[at], hist_sem.at[g])

    def build_cols(b, carry):
        high, low = column_band(b, span_re, span_im, swing_re, swing_im)
        high, low = split(dot3(x_hi[...], x_lo[...], high, low))
        y[0, b] = high
        y[1, b] = low
        y_copy(0, b).start()
        y_copy(1, b).start()
        return carry

    lax.fori_loop(0, bands, build_cols, 0, unroll=2)

    reads[2].wait()
    reads[3].wait()
    hist[blocks] = jnp.zeros((24, 128), f32)
    spare = pltpu.make_async_copy(hist.at[pl.ds(blocks, 1)], hist_out.at[pl.ds(blocks, 1)], spare_sem)
    spare.start()
    rows8 = lax.broadcasted_iota(jnp.int32, (8, 128), 0)
    rows128 = lax.broadcasted_iota(jnp.int32, (128, 128), 0)

    def count_cells(g, carry):
        base = pl.multiple_of(g * GROUP, GROUP)
        q = cells[pl.ds(base, GROUP), :]
        qr = q // TILE_C
        qc = q - qr * TILE_C
        parts = []
        for p in range(2):
            v = vis[p, pl.ds(base, GROUP), :]
            high = v.astype(bf16).astype(f32)
            parts += [high, v - high]
        for s in range(GROUP):
            row = (rows8 == qr[s : s + 1]).astype(f32)
            pieces = [row] + [row * part[s : s + 1] for part in parts]
            lhs = jnp.concatenate(pieces + [jnp.zeros((8, 128), f32)], axis=0).astype(bf16)
            hot = (rows128 == qc[s : s + 1]).astype(f32).astype(bf16)
            out = nt(lhs, hot)
            hist[base + s, 0:8] = out[0:8]
            hist[base + s, 8:16] = out[8:16] + out[16:24]
            hist[base + s, 16:24] = out[24:32] + out[32:40]
        hist_copy(g).start()
        return carry

    groups = (live[0] + GROUP - 1) // GROUP
    lax.fori_loop(0, groups, count_cells, 0)

    def hist_wait(g, carry):
        hist_copy(g).wait()
        return carry

    lax.fori_loop(0, groups, hist_wait, 0)
    spare.wait()
    for part in range(2):
        for b in range(bands):
            y_copy(part, b).wait()


def adjoint_kernel(
    sizes, entries, bands_of, image_in, y_in, hist_in, table_in,
    out, image, y, hist, table, sems, wt_hi, wt_lo, z, acc, r_ref, *sets,
):
    side = image.shape[0]
    bands = y.shape[1]
    chunks = entries.shape[0] // GROUP
    reads = [
        pltpu.make_async_copy(source, to, sems.at[i])
        for i, (source, to) in enumerate(((table_in, table), (y_in, y), (hist_in, hist), (image_in, image)))
    ]
    for read in reads:
        read.start()
    span_re, span_im, swing_re, swing_im, turn_re, turn_im, near_re, near_im = table_views(table, sizes)
    reads[0].wait()
    tall = wt_hi.shape[0]
    sets = (sets[:3], sets[3:])

    def build_rows(a, carry):
        pr = jnp.broadcast_to(turn_re[pl.ds(a, 1), :], (8, 128))
        pi = jnp.broadcast_to(turn_im[pl.ds(a, 1), :], (8, 128))
        for t in range(side // 128):
            at = slice(t * 128, (t + 1) * 128)
            nr, ni = near_re[8 * t : 8 * t + 8], near_im[8 * t : 8 * t + 8]
            both = jnp.concatenate([pr * nr - pi * ni, pr * ni + pi * nr], axis=0)
            high, low = split(both)
            wt_hi[a, :, at] = high
            wt_lo[a, :, at] = low
        return carry

    lax.fori_loop(0, tall, build_rows, 0, unroll=4)
    z[...] = jnp.zeros_like(z)
    for read in reads[1:]:
        read.wait()

    def evaluate(c, refs):
        wg_hi, wg_lo, o_ref = refs
        b = bands_of[c]
        for s in range(GROUP):
            a = entries[c * GROUP + s] & 127
            wg_hi[16 * s : 16 * s + 16] = wt_hi[a]
            wg_lo[16 * s : 16 * s + 16] = wt_lo[a]
        o_ref[...] = dot3(wg_hi[...], wg_lo[...], y[0, b], y[1, b])

    def spread(c, refs):
        wg_hi, wg_lo, o_ref = refs
        for s in range(GROUP):
            k = entries[c * GROUP + s] // 128
            top = slice(16 * s, 16 * s + 8)
            low = slice(16 * s + 8, 16 * s + 16)
            model_re = o_ref[top, 0:128] - o_ref[low, 128:256]
            model_im = o_ref[top, 128:256] + o_ref[low, 0:128]
            many = hist[k, 0:8]
            g_re = many * model_re - hist[k, 8:16]
            g_im = many * model_im - hist[k, 16:24]
            r_ref[top, 0:128] = g_re
            r_ref[top, 128:256] = g_im
            r_ref[low, 0:128] = g_im
            r_ref[low, 128:256] = -g_re
        rt_hi, rt_lo = split(r_ref[...].T)
        z[bands_of[c]] += dot3(rt_hi, rt_lo, wg_hi[...], wg_lo[...])

    evaluate(0, sets[0])

    def work(i, carry):
        evaluate(2 * i + 1, sets[1])
        spread(2 * i, sets[0])
        evaluate(2 * i + 2, sets[0])
        spread(2 * i + 1, sets[1])
        return carry

    lax.fori_loop(0, (bands_of[chunks] + 1) // 2, work, 0)
    acc[...] = jnp.zeros_like(acc)

    def back(b, carry):
        wc_hi, wc_lo = column_band(b, span_re, span_im, swing_re, swing_im)
        high, low = split(z[b])
        acc[...] += dot3(wc_hi, wc_lo, high, low)
        return carry

    lax.fori_loop(0, bands, back, 0, unroll=2)
    out[...] = image[...] - tau_step * acc[...].T


def whole(n):
    return [pl.BlockSpec(memory_space=pltpu.VMEM) for _ in range(n)]


def in_hbm(n):
    return [pl.BlockSpec(memory_space=pltpu.HBM) for _ in range(n)]


def forward(plane, vis, cells, count, table, sizes):
    side = plane.shape[0]
    bands = 2 * side // TILE_C
    blocks = cells.shape[0]
    y = (2, bands, side, 256)
    hist = (blocks + 1, 24, 128)
    return pl.pallas_call(
        functools.partial(forward_kernel, sizes[:4]),
        out_shape=[jax.ShapeDtypeStruct(y, bf16), jax.ShapeDtypeStruct(hist, f32)],
        grid_spec=pltpu.PrefetchScalarGridSpec(
            num_scalar_prefetch=1,
            grid=(),
            in_specs=in_hbm(4),
            out_specs=in_hbm(2),
            scratch_shapes=[
                pltpu.VMEM(plane.shape, f32),
                pltpu.VMEM(cells.shape, jnp.int32),
                pltpu.VMEM(vis.shape, f32),
                pltpu.VMEM((sum(sizes[:4]), 128), f32),
                pltpu.VMEM(y, bf16),
                pltpu.VMEM(hist, f32),
                pltpu.VMEM((side, side), bf16),
                pltpu.VMEM((side, side), bf16),
                pltpu.SemaphoreType.DMA((4,)),
                pltpu.SemaphoreType.DMA((2, bands)),
                pltpu.SemaphoreType.DMA((blocks // GROUP,)),
                pltpu.SemaphoreType.DMA,
            ],
        ),
        compiler_params=pltpu.CompilerParams(vmem_limit_bytes=BIG),
        name="forward",
    )(count, plane, cells, vis, table)


def adjoint(entries, bands_of, plane, y, hist, table, sizes):
    _, bands, side, _ = y.shape
    tall = 2 * side // TILE_R
    buffers = [pltpu.VMEM((256, side), bf16), pltpu.VMEM((256, side), bf16), pltpu.VMEM((256, 256), f32)]
    return pl.pallas_call(
        functools.partial(adjoint_kernel, sizes),
        out_shape=jax.ShapeDtypeStruct((side, side), f32),
        grid_spec=pltpu.PrefetchScalarGridSpec(
            num_scalar_prefetch=2,
            grid=(),
            in_specs=in_hbm(4),
            out_specs=whole(1)[0],
            scratch_shapes=[
                pltpu.VMEM(plane.shape, f32),
                pltpu.VMEM(y.shape, bf16),
                pltpu.VMEM(hist.shape, f32),
                pltpu.VMEM(table.shape, f32),
                pltpu.SemaphoreType.DMA((4,)),
                pltpu.VMEM((tall, 16, side), bf16),
                pltpu.VMEM((tall, 16, side), bf16),
                pltpu.VMEM((bands, 256, side), f32),
                pltpu.VMEM((side, side), f32),
                pltpu.VMEM((256, 256), f32),
            ]
            + buffers * 2,
        ),
        compiler_params=pltpu.CompilerParams(vmem_limit_bytes=BIG),
        name="adjoint",
    )(entries, bands_of, plane, y, hist, table)


def gram_kernel(even, dual, image, first, second):
    channels = first.shape[0]
    side = image.shape[1]
    rows = image.shape[0] // channels
    at = jnp.where(even[0] == 1, rows - 1, 0)
    for c in range(channels):
        first[c : c + 1, :side] = image[pl.ds(c * rows + at, 1), :]
        second[c : c + 1] = image[pl.ds(c * rows + rows - 1 - at, 1), :]
    first[:, side:] = jnp.zeros((channels, first.shape[1] - side), f32)
    pick, match = row_maps(dual.shape[0], channels)
    high, low = split(dual[...] + sigma_step * image[...])
    full = jnp.where(match, nt(high, high) + nt(high, 2.0 * low), 0.0)
    half = sum(
        lax.dot_general(pick, part, (((0,), (0,)), ((), ())), preferred_element_type=f32)
        for part in split(full)
    )
    gram = sum(jnp.dot(part, pick, preferred_element_type=f32) for part in split(half))
    first[:, side : side + channels] = 0.5 * (gram + gram.T)


def packing(rows, side):
    short = 8 if rows % 8 == 0 else rows
    return short, rows // short * side, 2 * side // short


def dual_kernel(ridge, bound, even, *refs):
    *grams, image, flat_image, first, second, dual, low = refs[:-11]
    wavelet_out, lowrank_out, packed_out = refs[-11:-8]
    wavelet, lowrank, packed, beside, b_hi, b_lo, result, out_sem = refs[-8:]
    channels, rows, side = image.shape
    short, wide, spare = packing(rows, side)
    total = channels * rows
    step_rows = total // PARTS
    step_channels = channels // PARTS
    one_way, other_way = first[:, :side], second[...]
    beside[0] = jnp.where(even[0] == 1, other_way, one_way)
    beside[1] = jnp.where(even[0] == 1, one_way, other_way)

    def copy(which, part):
        source, to = ((packed, packed_out), (wavelet, wavelet_out), (lowrank, lowrank_out))[which]
        at = pl.ds(part * step_channels, step_channels)
        return pltpu.make_async_copy(source.at[at], to.at[at], out_sem.at[which, part])

    def details(part):
        for c in range(part * step_channels, (part + 1) * step_channels):
            w = dual[c]
            b = bound[c]
            step = columns(rows_between(image[c], beside[0, c : c + 1], beside[1, c : c + 1]))
            new = jnp.clip(w + sigma_step * step, -b, b)
            wavelet[c] = new
            slope = columns(tau_step * (2.0 * new - w))
            own = rows_between(slope, 0.0, 0.0)
            for h in range(rows // short):
                packed[c, :, h * side : (h + 1) * side] = own[h * short : (h + 1) * short]
            for k in range(short // 2):
                lanes = slice(k * spare, (k + 1) * spare)
                packed[c, k : k + 1, wide:] = -0.5 * slope[:1, lanes]
                packed[c, short // 2 + k : short // 2 + k + 1, wide:] = -0.5 * slope[rows - 1 :, lanes]

    pick, match = row_maps(total, channels)
    b_hi[...], b_lo[...] = split(low[...] + sigma_step * flat_image[...])
    gram = grams[0][...]
    for other in grams[1:]:
        gram = gram + other[...]
    ci = lax.broadcasted_iota(jnp.int32, (channels, channels), 0)
    cj = lax.broadcasted_iota(jnp.int32, (channels, channels), 1)
    identity = (ci == cj).astype(f32)
    shifted = gram + ridge * identity
    trace = jnp.sum(shifted * identity, keepdims=True)
    current = shifted / trace
    factor = 1.5 * identity - 0.5 * current
    inverse = factor
    for turn in range(1, NS_STEPS):
        current = jnp.dot(current, factor, precision=highest)
        if turn <= PARTS:
            details(turn - 1)
        factor = 1.5 * identity - 0.5 * jnp.dot(inverse, current, precision=highest)
        inverse = jnp.dot(factor, inverse, precision=highest)
    for part in range(NS_STEPS - 1, PARTS):
        details(part)
    for part in range(PARTS):
        copy(1, part).start()
    root_hi, root_lo = split(inverse * (math.sqrt(ridge) * lax.rsqrt(trace)))
    half = total // HALVES

    for h in range(HALVES):
        at = slice(h * half, (h + 1) * half)

        def spread(x):
            narrow = jnp.dot(pick[at], x, preferred_element_type=f32).astype(bf16)
            return jnp.where(match[at], nt(narrow, pick), 0.0).astype(bf16)

        result[...] = dot3(spread(root_hi), spread(root_lo), b_hi[...], b_lo[...])
        for part in range(h * PARTS // HALVES, (h + 1) * PARTS // HALVES):
            for c in range(part * step_channels, (part + 1) * step_channels):
                mine = result[c * rows - h * half : (c + 1) * rows - h * half]
                lowrank[c] = mine
                more = tau_step * (2.0 * mine - low[c * rows : (c + 1) * rows])
                for i in range(rows // short):
                    packed[c, :, i * side : (i + 1) * side] += more[i * short : (i + 1) * short]
            copy(0, part).start()
            copy(2, part).start()
    for which in range(3):
        for part in range(PARTS):
            copy(which, part).wait()


def shift_lanes(x):
    wide = x.shape[-1]
    lane = lax.broadcasted_iota(jnp.int32, x.shape, 1)
    before = jnp.where(lane == 0, 0.0, pltpu.roll(x, 1, 1))
    after = jnp.where(lane == wide - 1, 0.0, pltpu.roll(x, wide - 1, 1))
    return before + after


def columns(x):
    return x - 0.5 * shift_lanes(x)


def rows_between(x, above, below):
    height = x.shape[0]
    row = lax.broadcasted_iota(jnp.int32, x.shape, 0)
    up = jnp.where(row == 0, above, pltpu.roll(x, 1, 0))
    down = jnp.where(row == height - 1, below, pltpu.roll(x, height - 1, 0))
    return x - 0.5 * (up + down)


def row_maps(total, channels, start=0, count=None):
    rows = total // channels
    count = total if count is None else count
    si = lax.broadcasted_iota(jnp.int32, (count, channels), 0) + start
    sj = lax.broadcasted_iota(jnp.int32, (count, channels), 1)
    pick = ((si >= sj * rows) & (si < sj * rows + rows)).astype(f32).astype(bf16)
    i = lax.rem(lax.broadcasted_iota(jnp.int32, (count, 1), 0), rows)
    j = lax.rem(lax.broadcasted_iota(jnp.int32, (1, total), 1), rows)
    return pick, i == j


def local_gram(even, dual, image, channels):
    lanes = image.shape[1] + -(-channels // 128) * 128
    return pl.pallas_call(
        gram_kernel,
        out_shape=[jax.ShapeDtypeStruct((channels, n), f32) for n in (lanes, image.shape[1])],
        in_specs=[pl.BlockSpec(memory_space=pltpu.SMEM)] + whole(2),
        out_specs=whole(2),
        compiler_params=pltpu.CompilerParams(vmem_limit_bytes=12 * MIB),
        name="gram",
    )(even, dual, image)


def final_kernel(base_in, sent, out_ref, base, base_sem, out_sem):
    devices, short, _ = sent.shape
    side = base.shape[1]
    rows = base.shape[0] // devices
    _, wide, spare = packing(rows, side)
    step = devices // PIECES

    def read(part):
        at = pl.ds(part * step * rows, step * rows)
        return pltpu.make_async_copy(base_in.at[at], base.at[at], base_sem.at[part])

    def write(part):
        at = pl.ds(part * step * rows, step * rows)
        return pltpu.make_async_copy(base.at[at], out_ref.at[at], out_sem.at[part])

    def beside(d, first):
        return jnp.concatenate([sent[d, first + k : first + k + 1, wide:] for k in range(short // 2)], axis=1)

    for part in range(PIECES):
        read(part).start()
    row = lax.broadcasted_iota(jnp.int32, (short, side), 0)
    for part in range(PIECES):
        read(part).wait()
        for d in range(part * step, (part + 1) * step):
            for h in range(rows // short):
                at = slice(d * rows + h * short, d * rows + (h + 1) * short)
                left = base[at] - sent[d, :, h * side : (h + 1) * side]
                if h == 0 and d > 0:
                    left = jnp.where(row == 0, left - beside(d - 1, short // 2), left)
                if (h + 1) * short == rows and d + 1 < devices:
                    left = jnp.where(row == short - 1, left - beside(d + 1, 0), left)
                base[at] = jnp.maximum(left, 0.0)
        write(part).start()
    for part in range(PIECES):
        write(part).wait()


def final_image(base, sent):
    return pl.pallas_call(
        final_kernel,
        out_shape=jax.ShapeDtypeStruct(base.shape, f32),
        in_specs=in_hbm(1) + whole(1),
        out_specs=in_hbm(1)[0],
        scratch_shapes=[pltpu.VMEM(base.shape, f32)] + [pltpu.SemaphoreType.DMA((PIECES,))] * 2,
        input_output_aliases={0: 0},
        compiler_params=pltpu.CompilerParams(vmem_limit_bytes=8 * MIB),
        name="final",
    )(base, sent)


def dual_update(ridge, bound, even, grams, image, first, second, dual, low):
    channels, rows, side = image.shape
    flat = (channels * rows, side)
    short, wide, spare = packing(rows, side)
    packed = (channels, short, wide + spare)
    smem = pl.BlockSpec(memory_space=pltpu.SMEM)
    return pl.pallas_call(
        functools.partial(dual_kernel, ridge),
        out_shape=[jax.ShapeDtypeStruct(image.shape, f32)] * 2 + [jax.ShapeDtypeStruct(packed, f32)],
        in_specs=[smem, smem] + whole(len(grams) + 6),
        out_specs=in_hbm(3),
        scratch_shapes=[
            pltpu.VMEM(image.shape, f32),
            pltpu.VMEM(image.shape, f32),
            pltpu.VMEM(packed, f32),
            pltpu.VMEM((2, channels, side), f32),
            pltpu.VMEM(flat, bf16),
            pltpu.VMEM(flat, bf16),
            pltpu.VMEM((flat[0] // HALVES, side), f32),
            pltpu.SemaphoreType.DMA((3, PARTS)),
        ],
        compiler_params=pltpu.CompilerParams(vmem_limit_bytes=24 * MIB),
        name="dual",
    )(bound, even, *grams, image, image.reshape(flat), first, second, dual, low.reshape(flat))


def per_device(
    image, visibilities, tile_index, cells, block_count, lowrank_dual, wavelet_dual, wavelet_bound
):
    side = image.shape[-1]
    channels, rows_here, _ = lowrank_dual.shape
    devices = lax.axis_size(RING)
    pieces = lax.axis_size("pix")
    flat = (channels * rows_here, side)

    facet_image = lax.all_to_all(
        image.reshape(devices, rows_here, side), RING, split_axis=0, concat_axis=0, tiled=True
    )

    bands = 2 * side // TILE_C
    chunks = tile_index.shape[1] // GROUP + bands + 1
    table, sizes = small_tables(side, side)
    table = jnp.asarray(table)
    entries, bands_of = plan_blocks(tile_index[0], block_count[0], bands, chunks)
    y, hist = forward(image[0], visibilities[:, 0], cells[0], block_count, table, sizes)
    even = (1 - lax.axis_index(RING) % 2).astype(jnp.int32)[None]
    facet_image, y, entries, bands_of, even = lax.optimization_barrier(
        (facet_image, y, entries, bands_of, even)
    )

    inner = [(i, i + 1) for i in range(1, devices - 1, 2)]
    first, second = local_gram(even, lowrank_dual.reshape(flat), facet_image.reshape(flat), channels)
    second_got = lax.ppermute(second, RING, inner + [(j, i) for i, j in inner])
    first_got = lax.ppermute(first, RING, [(i, i ^ 1) for i in range(devices)])
    grams = [first[:, side : side + channels], first_got[:, side : side + channels]]
    for turn in range(1, pieces.bit_length() - 1):
        gram = sum(grams)
        grams = [gram, lax.ppermute(gram, "pix", [(i, i ^ (1 << turn)) for i in range(pieces)])]
    ridge = float(rows_here * side * pieces)
    wavelet_next, lowrank_next, packed = dual_update(
        ridge, wavelet_bound, even, grams, facet_image, first_got, second_got, wavelet_dual, lowrank_dual
    )
    packed, y = lax.optimization_barrier((packed, y))
    returned = lax.all_to_all(packed, RING, split_axis=0, concat_axis=0, tiled=True)
    base = adjoint(entries, bands_of, image[0], y, hist, table, sizes)
    image_next = final_image(base, returned)
    return (image_next[None], lowrank_next, wavelet_next)


def solution(mesh):
    return jax.shard_map(
        per_device,
        mesh=mesh,
        in_specs=(
            P(RING, None, None),
            P(None, RING, None, None),
            P(RING, None),
            P(RING, None, None),
            P(RING),
            P(None, RING, None),
            P(None, RING, None),
            P(),
        ),
        out_specs=(P(RING, None, None), P(None, RING, None), P(None, RING, None)),
        check_vma=False,
    )
```
